32 devices in a mesh: dp: 2 (over y), seq: 4 (over x, core), fsdp: 4 (over z).
Axes of the slice: x: 2, y: 2, z: 4, core: 2. Of those that a mesh axis runs over, the one named last changes fastest.
Arguments:
- tokens: bfloat16 [4096, 2048], P(('dp', 'seq', 'fsdp')), may hold values from -6 to 6
- mixer_gain: float32 [2048], replicated, may hold values from 0.25 to 1.75
- mixer_shift: float32 [2048], replicated, may hold values from -3 to 3
- w_query: bfloat16 [2048, 2048], P('fsdp'), may hold values from -0.125 to 0.125
- w_key: bfloat16 [2048, 2048], P('fsdp'), may hold values from -0.125 to 0.125
- w_value: bfloat16 [2048, 4096], P('fsdp'), may hold values from -0.125 to 0.125
- w_gate: bfloat16 [2048, 4096], P('fsdp'), may hold values from -0.125 to 0.125
- decay_exponent: int32 [8], replicated, may hold values from 5 to 13
- group_gain: float32 [4096], replicated, may hold values from 0.25 to 1.75
- group_shift: float32 [4096], replicated, may hold values from -3 to 3
- w_out: bfloat16 [4096, 2048], P('fsdp'), may hold values from -0.1875 to 0.1875
- feed_gain: float32 [2048], replicated, may hold values from 0.25 to 1.75
- feed_shift: float32 [2048], replicated, may hold values from -3 to 3
- w_act: bfloat16 [2048, 4096], P('fsdp'), may hold values from -0.125 to 0.125
- w_lin: bfloat16 [2048, 4096], P('fsdp'), may hold values from -0.125 to 0.125
- w_down: bfloat16 [4096, 2048], P('fsdp'), may hold values from -0.1875 to 0.1875
- cotangent: bfloat16 [4096, 2048], P(('dp', 'seq', 'fsdp')), may hold values from -6 to 6
Outputs:
- result: bfloat16 [4096, 2048], P(('dp', 'seq', 'fsdp'))
- grad_tokens: bfloat16 [4096, 2048], P(('dp', 'seq', 'fsdp'))
- grad_query: float32 [2048, 2048], P('fsdp')
- grad_key: float32 [2048, 2048], P('fsdp')
- grad_value: float32 [2048, 4096], P('fsdp')
- grad_gate: float32 [2048, 4096], P('fsdp')
- grad_out: float32 [4096, 2048], P('fsdp')
- grad_act: float32 [2048, 4096], P('fsdp')
- grad_lin: float32 [2048, 4096], P('fsdp')
- grad_down: float32 [4096, 2048], P('fsdp')
- grad_mixer_gain: float32 [2048], replicated
- grad_mixer_shift: float32 [2048], replicated
- grad_group_gain: float32 [4096], replicated
- grad_group_shift: float32 [4096], replicated
- grad_feed_gain: float32 [2048], replicated
- grad_feed_shift: float32 [2048], replicated
The draws below stay inside these ranges and needn't reach their ends.
All inputs are finite; a program needn't handle non-finite values.
Results may differ from the reference program's by a relative error of at most 0.028.
The reference program's roundings to bfloat16 on the way count: a program that leaves them out, or rounds other values in their place, can miss the bound.
Values may be sent and summed in bfloat16 or wider, within the bound.
No kernel may reach another device: no remote copies, remote signals or barrier semaphores. Data moves between devices by JAX's collectives and lax.ppermute only.
A program may use at most 576 MiB of HBM per device.

```python
from functools import partial
import jax
import jax.numpy as jnp
from jax import lax

D = 2048
H = 8
KD = 256
VD = 512
FF = 4096
SPAN = 512
SEQ_LEN = 2048
TOKENS = 4096
N_DP = 2


def set_ends(values, key, low, high):
    extent = values.shape
    index_at = [jax.random.randint(jax.random.fold_in(key, axis), (), 0, extent[axis]) for axis in range(len(extent))]
    values = values.at[tuple(index_at)].set(low)
    longest = extent.index(max(extent))
    index_at[longest] = (index_at[longest] + 1) % extent[longest]
    return values.at[tuple(index_at)].set(high)


def block_levels(rng, dims, cuts, low, top_value):
    factor_of, own = 1.0, jax.random.fold_in(rng, 6)
    for axis_at, shards_of in cuts:
        heights = jnp.exp(jax.random.uniform(jax.random.fold_in(own, axis_at), (shards_of,), jnp.float32, low / len(cuts), top_value / len(cuts)))
        factor_of = factor_of * jnp.repeat(heights, dims[axis_at] // shards_of).reshape([-1 if axis == axis_at else 1 for axis in range(len(dims))])
    return factor_of


def scatter_about(key, shape, scale, bound, split=(), held_as=jnp.bfloat16):
    level = block_levels(key, shape, split, -0.22, 0.18) if split else 1.0
    entries = jax.random.normal(key, shape, jnp.float32) * scale * level
    return jnp.minimum(jnp.maximum(entries, -bound), bound).astype(held_as)


def setup_inputs(seed: int = 0) -> dict:
    splits = jax.random.split(jax.random.key(seed), 18)
    return {
        "tokens": scatter_about(splits[0], (TOKENS, D), 1.0, 6.0, ((0, 32),)),
        "mixer_gain": jnp.clip(1.0 + 0.15 * jax.random.normal(splits[1], (D,), jnp.float32), 0.25, 1.75),
        "mixer_shift": scatter_about(splits[2], (D,), 0.5, 3.0, (), jnp.float32),
        "w_query": scatter_about(splits[3], (D, H * KD), D ** -0.5, 0.125, ((0, 4),)),
        "w_key": scatter_about(splits[4], (D, H * KD), D ** -0.5, 0.125, ((0, 4),)),
        "w_value": scatter_about(splits[5], (D, H * VD), D ** -0.5, 0.125, ((0, 4),)),
        "w_gate": scatter_about(splits[6], (D, H * VD), D ** -0.5, 0.125, ((0, 4),)),
        "decay_exponent": set_ends(jax.random.randint(splits[7], (H,), 5, 14), jax.random.fold_in(splits[7], 1), 5, 13).astype(jnp.int32),
        "group_gain": jnp.clip(1.0 + 0.15 * jax.random.normal(splits[8], (H * VD,), jnp.float32), 0.25, 1.75),
        "group_shift": scatter_about(splits[9], (H * VD,), 0.5, 3.0, (), jnp.float32),
        "w_out": scatter_about(splits[10], (H * VD, D), (H * VD // 4) ** -0.5, 0.1875, ((0, 4),)),
        "feed_gain": jnp.clip(1.0 + 0.15 * jax.random.normal(splits[11], (D,), jnp.float32), 0.25, 1.75),
        "feed_shift": scatter_about(splits[12], (D,), 0.5, 3.0, (), jnp.float32),
        "w_act": scatter_about(splits[13], (D, FF), D ** -0.5, 0.125, ((0, 4),)),
        "w_lin": scatter_about(splits[14], (D, FF), D ** -0.5, 0.125, ((0, 4),)),
        "w_down": scatter_about(splits[15], (FF, D), (FF // 4) ** -0.5, 0.1875, ((0, 4),)),
        "cotangent": scatter_about(splits[16], (TOKENS, D), 1.0, 6.0, ((0, 32),)),
    }


@jax.custom_vjp
def low(v):
    return lax.optimization_barrier(v.astype(jnp.bfloat16)).astype(jnp.float32)

@jax.custom_vjp
def low_back(v):
    return v

def low_keep(v):
    return (low(v), None)

def low_pass(kept, grad):
    return (grad,)

def back_keep(v):
    return (v, None)

def back_low(kept, grad):
    return (low(grad),)
low.defvjp(low_keep, low_pass)
low_back.defvjp(back_keep, back_low)
EPSILON = 1e-05

def rounded_both(values):
    return low(low_back(values))

def matmul_high(left, right):
    return jnp.dot(left, right, precision=lax.Precision.HIGHEST)

def layer_norm(values, gain, shift):
    center = values - lax.optimization_barrier(jnp.mean(values, -1, keepdims=True))
    spread = lax.optimization_barrier(jnp.mean(center * center, -1, keepdims=True))
    return center * lax.rsqrt(spread + EPSILON) * gain + shift

def decay_tables(log_rate):
    positions = jnp.arange(SPAN).astype(jnp.float32)
    offsets = positions[:, None] - positions[None, :]
    key_scale = KD ** (-0.5)
    inside = jnp.where(offsets[None] >= 0, jnp.exp(jnp.maximum(offsets, 0.0)[None] * log_rate[:, None, None]), 0.0) * key_scale
    query_factor = key_scale * jnp.exp((positions + 1.0)[:, None] * log_rate[None, :])
    key_factor = jnp.exp((SPAN - 1.0 - positions)[:, None] * log_rate[None, :])
    carry_factor = jnp.exp(SPAN * log_rate)
    return (inside, query_factor, key_factor, carry_factor)

def retention(queries, key_rows, value_rows, tables):
    inside, query_factor, key_factor, carry_factor = tables
    block_count = queries.shape[0] // SPAN
    query_blocks = queries.reshape(block_count, SPAN, H, KD)
    key_blocks = key_rows.reshape(block_count, SPAN, H, KD)
    value_blocks = value_rows.reshape(block_count, SPAN, H, VD)

    def block_step(state, block):
        query_block, key_block, value_block = block
        scores = low_back(jnp.einsum('ihd,jhd->hij', query_block, key_block, precision=lax.Precision.HIGHEST))
        masked = low(scores * inside)
        output = jnp.einsum('hij,jhe->ihe', masked, value_block, precision=lax.Precision.HIGHEST)
        output = output + jnp.einsum('ihd,hde->ihe', query_block * query_factor[:, :, None], state, precision=lax.Precision.HIGHEST)
        update = jnp.einsum('jhd,jhe->hde', key_block * key_factor[:, :, None], value_block, precision=lax.Precision.HIGHEST)
        return (state * carry_factor[:, None, None] + update, output)
    initial = jnp.zeros((H, KD, VD), jnp.float32)
    outputs = lax.scan(jax.checkpoint(block_step), initial, (query_blocks, key_blocks, value_blocks))[1]
    return outputs.reshape(queries.shape[0], H, VD)

def reference(tokens, mixer_gain, mixer_shift, w_query, w_key, w_value, w_gate, decay_exponent, group_gain, group_shift, w_out, feed_gain, feed_shift, w_act, w_lin, w_down, cotangent):
    log_rate = jnp.log1p(-jnp.exp2(-decay_exponent.astype(jnp.float32)))
    tables = decay_tables(log_rate)

    def forward(inputs, m_gain, m_shift, wq_all, wk_all, wv_all, wg_all, g_gain, g_shift, wo_all, f_gain, f_shift, wa_all, wl_all, wd_all):
        normed = low(layer_norm(inputs, m_gain, m_shift))
        queries = rounded_both(matmul_high(normed, wq_all)).reshape(N_DP, SEQ_LEN, H, KD)
        key_rows = rounded_both(matmul_high(normed, wk_all)).reshape(N_DP, SEQ_LEN, H, KD)
        value_rows = rounded_both(matmul_high(normed, wv_all)).reshape(N_DP, SEQ_LEN, H, VD)
        gate_pre = low_back(matmul_high(normed, wg_all))
        mixed = low_back(jax.vmap(partial(retention, tables=tables))(queries, key_rows, value_rows))
        center_mean = lax.optimization_barrier(jnp.mean(mixed, -1, keepdims=True))
        square_mean = lax.optimization_barrier(jnp.mean(mixed * mixed, -1, keepdims=True))
        normal = (mixed - center_mean) * lax.rsqrt(square_mean - center_mean * center_mean + EPSILON)
        headed = rounded_both(normal).reshape(TOKENS, H * VD)
        gated = low(jax.nn.silu(gate_pre) * (headed * g_gain + g_shift))
        middle = inputs + low_back(matmul_high(gated, wo_all))
        second = low(layer_norm(middle, f_gain, f_shift))
        active = low_back(matmul_high(second, wa_all))
        linear = low_back(matmul_high(second, wl_all))
        hidden = low(jax.nn.gelu(active, approximate=False) * linear)
        return middle + low_back(matmul_high(hidden, wd_all))
    result, pullback = jax.vjp(forward, tokens.astype(jnp.float32), mixer_gain, mixer_shift, w_query.astype(jnp.float32), w_key.astype(jnp.float32), w_value.astype(jnp.float32), w_gate.astype(jnp.float32), group_gain, group_shift, w_out.astype(jnp.float32), feed_gain, feed_shift, w_act.astype(jnp.float32), w_lin.astype(jnp.float32), w_down.astype(jnp.float32))
    grads = pullback(cotangent.astype(jnp.float32))
    return (result.astype(jnp.bfloat16), grads[0].astype(jnp.bfloat16), grads[3], grads[4], grads[5], grads[6], grads[9], grads[12], grads[13], grads[14], grads[1], grads[2], grads[7], grads[8], grads[10], grads[11])
```

```python
import jax
import jax.numpy as jnp
from jax import lax
from jax.sharding import PartitionSpec as P

H = 8
KD = 256
VD = 512
SPAN = 512
EPSILON = 1e-05
BF = jnp.bfloat16
F32 = jnp.float32


def norm_parts(values):
    center = values - jnp.mean(values, -1, keepdims=True)
    inverse = lax.rsqrt(jnp.mean(center * center, -1, keepdims=True) + EPSILON)
    return center * inverse, inverse


def norm_pull(scaled, inverse, gain, grad):
    lifted = grad * gain
    term = inverse * (
        lifted
        - jnp.mean(lifted, -1, keepdims=True)
        - scaled * jnp.mean(lifted * scaled, -1, keepdims=True)
    )
    return term, jnp.sum(grad * scaled, 0), jnp.sum(grad, 0)


def dot(left, right, left_axis, right_axis):
    return lax.dot_general(
        left, right, (((left_axis,), (right_axis,)), ((), ())), preferred_element_type=F32
    )


def shift(values, axis, step):
    count = lax.axis_size(axis)
    return lax.ppermute(values, axis, [(i, (i + step) % count) for i in range(count)])


def pass_on(values, axis, step):
    count = lax.axis_size(axis)
    pairs = [(i, i + step) for i in range(count) if 0 <= i + step < count]
    return lax.ppermute(values, axis, pairs)


def gather_rows(values):
    count = lax.axis_size("fsdp")
    return jnp.concatenate([values] + [shift(values, "fsdp", k) for k in range(1, count)], 0)


def scatter_rows(partial):
    count = lax.axis_size("fsdp")
    rows = partial.shape[0] // count
    low = partial.astype(BF)
    total = low[:rows].astype(F32)
    for k in range(1, count):
        total = total + shift(low[k * rows : (k + 1) * rows], "fsdp", -k).astype(F32)
    return total


def in_order(pieces, place):
    count = len(pieces)
    stacked = jnp.stack(pieces + pieces[:-1])
    return lax.dynamic_slice_in_dim(stacked, (count - place) % count, count, 0)


def replica_place():
    return lax.axis_index("dp") * lax.axis_size("seq") + lax.axis_index("seq")


def replica_count():
    return lax.axis_size("dp") * lax.axis_size("seq")


def column_weights(weights):
    count = lax.axis_size("fsdp")
    place = lax.axis_index("fsdp")
    rows = weights[0].shape[0] // replica_count()
    own = [lax.dynamic_slice_in_dim(w, replica_place() * rows, rows, 0) for w in weights]

    def piece(target):
        return jnp.concatenate(
            [
                lax.dynamic_slice_in_dim(
                    w, target * (w.shape[1] // count), w.shape[1] // count, 1
                )
                for w in own
            ],
            1,
        )

    pieces = [piece(place)]
    for k in range(1, count):
        pieces.append(shift(piece((place - k) % count), "fsdp", -k))
    mine = in_order(pieces, place)
    return lax.all_gather(
        mine.reshape(count * rows, mine.shape[2]), ("dp", "seq"), axis=0, tiled=True
    )


def row_grads(grad, widths):
    count = lax.axis_size("fsdp")
    place = lax.axis_index("fsdp")
    summed = lax.psum_scatter(grad.astype(BF), ("dp", "seq"), scatter_dimension=0, tiled=True)
    blocks = summed.reshape(count, summed.shape[0] // count, summed.shape[1])
    rows = blocks.shape[1]

    def piece(target):
        return lax.dynamic_index_in_dim(blocks, target, 0, False)

    pieces = [piece(place)]
    for k in range(1, count):
        pieces.append(shift(piece((place - k) % count), "fsdp", -k))
    mine = in_order(pieces, place)
    whole = lax.all_gather(
        mine.reshape(count * rows, mine.shape[2]), ("dp", "seq"), axis=0, tiled=True
    ).reshape(replica_count(), count, rows, mine.shape[2])
    outs, start = [], 0
    for width in widths:
        part = whole[:, :, :, start : start + width].transpose(0, 2, 1, 3)
        outs.append(part.reshape(replica_count() * rows, count * width).astype(F32))
        start += width
    return outs


def spread(values):
    rows, width = values.shape
    count, copies = lax.axis_size("fsdp"), replica_count()
    chunk = width // (count * copies)
    return values.reshape(rows, count, copies, chunk).transpose(0, 2, 1, 3).reshape(rows, width)


def unspread(values):
    rows, width = values.shape
    count, copies = lax.axis_size("fsdp"), replica_count()
    chunk = width // (count * copies)
    return values.reshape(rows, copies, count, chunk).transpose(0, 2, 1, 3).reshape(rows, width)


def prefix_states(own, decay, sign):
    count = lax.axis_size("seq")
    low = own.astype(BF)
    total = pass_on(low, "seq", sign).astype(F32)
    for k in range(2, count):
        total = total + pass_on(low, "seq", sign * k).astype(F32) * decay ** (k - 1)
    return total


def on_device(
    tokens,
    mixer_gain,
    mixer_shift,
    w_query,
    w_key,
    w_value,
    w_gate,
    decay_exponent,
    group_gain,
    group_shift,
    w_out,
    feed_gain,
    feed_shift,
    w_act,
    w_lin,
    w_down,
    cotangent,
):
    count = lax.axis_size("fsdp")
    place = lax.axis_index("fsdp")
    rows = tokens.shape[0]
    group = rows * count
    spans = group // SPAN
    local_heads = H // count
    q_width, v_width = local_heads * KD, local_heads * VD
    h_width = w_act.shape[1] // count
    key_scale = KD ** (-0.5)

    def natural(values):
        if spans == 1:
            return values
        blocks = values.reshape(count, rows, values.shape[1])
        pieces = [blocks[0]] + [blocks[count - k] for k in range(1, count)]
        return in_order(pieces, place).reshape(values.shape)

    def relative(values):
        if spans == 1:
            return values
        blocks = values.reshape(count, rows, values.shape[1])
        doubled = jnp.concatenate([blocks, blocks[:-1]])
        turned = lax.dynamic_slice_in_dim(doubled, place, count, 0)
        return jnp.stack([turned[0]] + [turned[count - k] for k in range(1, count)]).reshape(
            values.shape
        )

    inputs = tokens.astype(F32)
    wide_in = column_weights((w_query, w_key, w_value, w_gate))
    scaled_in, inverse_in = norm_parts(inputs)
    normed = gather_rows(spread((scaled_in * mixer_gain + mixer_shift).astype(BF)))
    wide_feed = column_weights((w_act, w_lin))
    upstream = gather_rows(cotangent)

    log_rates = jnp.log1p(-jnp.exp2(-decay_exponent.astype(F32)))
    if spans == 1:
        index = jnp.arange(SPAN)
        source = (place - index // rows) % count
        positions = (source * rows + index % rows).astype(F32)
    else:
        positions = jnp.arange(SPAN).astype(F32)
    offsets = positions[:, None] - positions[None, :]

    projected = dot(normed, wide_in, 1, 0)
    queries = natural(projected[:, :q_width].astype(BF))
    keys = natural(projected[:, q_width : 2 * q_width].astype(BF))
    values = natural(projected[:, 2 * q_width : 2 * q_width + v_width].astype(BF))
    gate_pre = projected[:, 2 * q_width + v_width :]

    def head_slice(array, block, head, width):
        return array[block * SPAN : (block + 1) * SPAN, head * width : (head + 1) * width]

    tables = []
    for head in range(local_heads):
        log_rate = lax.dynamic_index_in_dim(log_rates, place * local_heads + head, 0, False)
        inside = (
            jnp.where(offsets >= 0, jnp.exp(jnp.maximum(offsets, 0.0) * log_rate), 0.0) * key_scale
        )
        tables.append(
            (
                inside,
                key_scale * jnp.exp((positions + 1.0) * log_rate)[:, None],
                jnp.exp((SPAN - 1.0 - positions) * log_rate)[:, None],
                jnp.exp(SPAN * log_rate),
            )
        )
    decays = jnp.stack([table[3] for table in tables])[:, None, None]

    local_states, finals = [], []
    for head in range(local_heads):
        _, _, key_factor, carry = tables[head]
        state, states = None, []
        for block in range(spans):
            scaled_keys = (
                head_slice(keys, block, head, KD).astype(F32) * key_factor
            ).astype(BF)
            update = dot(scaled_keys, head_slice(values, block, head, VD), 0, 0)
            states.append(state)
            state = update if state is None else state * carry + update
        local_states.append(states)
        finals.append(state)
    entering = prefix_states(jnp.stack(finals), decays**spans, 1)

    masked_all, state_all, normal_all, inv_all = [], [], [], []
    for head in range(local_heads):
        inside, query_factor, _, carry = tables[head]
        for block in range(spans):
            query = head_slice(queries, block, head, KD)
            value = head_slice(values, block, head, VD)
            masked = (dot(query, head_slice(keys, block, head, KD), 1, 1) * inside).astype(BF)
            state = entering[head] * carry**block
            if local_states[head][block] is not None:
                state = state + local_states[head][block]
            state_low = state.astype(BF)
            mixed = dot(masked, value, 1, 0) + query_factor * dot(query, state_low, 1, 0)
            mean = jnp.mean(mixed, -1, keepdims=True)
            inv_std = lax.rsqrt(jnp.mean(mixed * mixed, -1, keepdims=True) - mean * mean + EPSILON)
            masked_all.append(masked)
            state_all.append(state_low)
            normal_all.append((mixed - mean) * inv_std)
            inv_all.append(inv_std)

    def join(parts):
        return jnp.concatenate(
            [
                jnp.concatenate(parts[head * spans : (head + 1) * spans], 0)
                for head in range(local_heads)
            ],
            1,
        )

    headed = relative(join([normal.astype(BF) for normal in normal_all]))
    headed_wide = headed.astype(F32)
    gain = lax.dynamic_slice_in_dim(group_gain, place * v_width, v_width, 0)
    bias = lax.dynamic_slice_in_dim(group_shift, place * v_width, v_width, 0)
    sigmoid = jax.nn.sigmoid(gate_pre)
    silu = gate_pre * sigmoid
    scaled_heads = headed_wide * gain + bias
    gated = (silu * scaled_heads).astype(BF)

    middle = inputs + scatter_rows(dot(gated, w_out, 1, 0))
    scaled_mid, inverse_mid = norm_parts(middle)
    second = gather_rows(spread((scaled_mid * feed_gain + feed_shift).astype(BF)))
    both = dot(second, wide_feed, 1, 0)
    active, linear = both[:, :h_width], both[:, h_width:]
    cdf = 0.5 * (1.0 + lax.erf(active * (2.0**-0.5)))
    gelu = active * cdf
    hidden = (gelu * linear).astype(BF)
    hidden_grad = dot(upstream, w_down, 1, 1)
    slope = cdf + active * jnp.exp(-0.5 * active * active) * (0.5 / jnp.pi) ** 0.5
    feed_grads = jnp.concatenate(
        [(hidden_grad * linear * slope).astype(BF), (hidden_grad * gelu).astype(BF)], 1
    )
    second_grad = unspread(scatter_rows(dot(feed_grads, wide_feed, 1, 1)))
    result = (middle + scatter_rows(dot(hidden, w_down, 1, 0))).astype(BF)

    grad_down = lax.psum(dot(hidden, upstream, 0, 0).astype(BF), ("dp", "seq")).astype(F32)
    grad_act, grad_lin = row_grads(dot(second, feed_grads, 0, 0), (h_width, h_width))

    mid_term, grad_feed_gain, grad_feed_shift = norm_pull(
        scaled_mid, inverse_mid, feed_gain, second_grad
    )
    middle_grad = cotangent.astype(F32) + mid_term
    branch = gather_rows(middle_grad.astype(BF))
    gated_grad = dot(branch, w_out, 1, 1)
    grad_out = lax.psum(dot(gated, branch, 0, 0).astype(BF), ("dp", "seq")).astype(F32)

    gate_slope = sigmoid * (1.0 + gate_pre * (1.0 - sigmoid))
    gate_grad = (gated_grad * scaled_heads * gate_slope).astype(BF)
    shift_terms = gated_grad * silu
    grad_group_gain = jnp.sum(shift_terms * headed_wide, 0)
    grad_group_shift = jnp.sum(shift_terms, 0)
    headed_grad = natural((shift_terms * gain).astype(BF)).astype(F32)

    mixed_grads, terms = [], []
    for head in range(local_heads):
        _, query_factor, _, carry = tables[head]
        carried, later = None, [None] * spans
        for block in range(spans):
            at = head * spans + block
            upper = head_slice(headed_grad, block, head, VD)
            normal = normal_all[at]
            mixed_grads.append(
                (
                    inv_all[at]
                    * (
                        upper
                        - jnp.mean(upper, -1, keepdims=True)
                        - normal * jnp.mean(upper * normal, -1, keepdims=True)
                    )
                ).astype(BF)
            )
        for block in reversed(range(spans)):
            at = head * spans + block
            later[block] = carried
            scaled_query = (
                head_slice(queries, block, head, KD).astype(F32) * query_factor
            ).astype(BF)
            term = dot(scaled_query, mixed_grads[at], 0, 0)
            carried = term if carried is None else carried * carry + term
        terms.append((later, carried))
    leaving = prefix_states(jnp.stack([term[1] for term in terms]), decays**spans, -1)

    query_grads, key_grads, value_grads = [], [], []
    for head in range(local_heads):
        inside, query_factor, key_factor, carry = tables[head]
        for block in range(spans):
            at = head * spans + block
            query = head_slice(queries, block, head, KD)
            key = head_slice(keys, block, head, KD)
            value = head_slice(values, block, head, VD)
            carried = leaving[head] * carry ** (spans - 1 - block)
            if terms[head][0][block] is not None:
                carried = carried + terms[head][0][block]
            carried_low = carried.astype(BF)
            score_grad = (dot(mixed_grads[at], value, 1, 1) * inside).astype(BF)
            query_grads.append(
                (
                    dot(score_grad, key, 1, 0)
                    + query_factor * dot(mixed_grads[at], state_all[at], 1, 1)
                ).astype(BF)
            )
            key_grads.append(
                (
                    dot(score_grad, query, 0, 0) + key_factor * dot(value, carried_low, 1, 1)
                ).astype(BF)
            )
            value_grads.append(
                (
                    dot(masked_all[at], mixed_grads[at], 0, 0)
                    + key_factor * dot(key, carried_low, 1, 0)
                ).astype(BF)
            )
    in_grads = jnp.concatenate(
        [relative(join(query_grads)), relative(join(key_grads)), relative(join(value_grads)), gate_grad],
        1,
    )
    normed_grad = unspread(scatter_rows(dot(in_grads, wide_in, 1, 1)))
    grad_query, grad_key, grad_value, grad_gate = row_grads(
        dot(normed, in_grads, 0, 0), (q_width, q_width, v_width, v_width)
    )
    in_term, grad_mixer_gain, grad_mixer_shift = norm_pull(
        scaled_in, inverse_in, mixer_gain, normed_grad
    )
    grad_tokens = (middle_grad + in_term).astype(BF)

    def placed(part):
        return lax.dynamic_update_slice_in_dim(
            jnp.zeros(group_gain.shape, F32), part, place * v_width, 0
        )

    vectors = lax.psum(
        jnp.concatenate(
            [
                grad_mixer_gain,
                grad_mixer_shift,
                placed(grad_group_gain),
                placed(grad_group_shift),
                grad_feed_gain,
                grad_feed_shift,
            ]
        ),
        ("dp", "seq", "fsdp"),
    )
    width, wide = mixer_gain.shape[0], group_gain.shape[0]
    marks = [width, 2 * width, 2 * width + wide, 2 * width + 2 * wide, 3 * width + 2 * wide]
    small = jnp.split(vectors, marks)
    return (
        result,
        grad_tokens,
        grad_query,
        grad_key,
        grad_value,
        grad_gate,
        grad_out,
        grad_act,
        grad_lin,
        grad_down,
        *small,
    )


def solution(mesh):
    rows = P(("dp", "seq", "fsdp"), None)
    shard = P("fsdp", None)
    return jax.shard_map(
        on_device,
        mesh=mesh,
        in_specs=(
            rows,
            P(),
            P(),
            shard,
            shard,
            shard,
            shard,
            P(),
            P(),
            P(),
            shard,
            P(),
            P(),
            shard,
            shard,
            shard,
            rows,
        ),
        out_specs=(rows, rows) + (shard,) * 8 + (P(),) * 6,
        check_vma=False,
    )
```

```python
import jax
import jax.numpy as jnp
from jax import lax
from jax.experimental import pallas as pl
from jax.experimental.pallas import tpu as pltpu
from jax.sharding import PartitionSpec as P

H = 8
KD = 256
VD = 512
SPAN = 512
EPSILON = 1e-05
BF = jnp.bfloat16
F32 = jnp.float32


def norm_parts(values):
    center = values - jnp.mean(values, -1, keepdims=True)
    inverse = lax.rsqrt(jnp.mean(center * center, -1, keepdims=True) + EPSILON)
    return center * inverse, inverse


def norm_pull(scaled, inverse, gain, grad):
    lifted = grad * gain
    term = inverse * (
        lifted
        - jnp.mean(lifted, -1, keepdims=True)
        - scaled * jnp.mean(lifted * scaled, -1, keepdims=True)
    )
    return term, jnp.sum(grad * scaled, 0), jnp.sum(grad, 0)


def dot(left, right, left_axis, right_axis):
    return lax.dot_general(
        left, right, (((left_axis,), (right_axis,)), ((), ())), preferred_element_type=F32
    )


def after(values, *others):
    return lax.optimization_barrier((values, *others))[0]


def shift(values, axis, step):
    count = lax.axis_size(axis)
    return lax.ppermute(values, axis, [(i, (i + step) % count) for i in range(count)])


def pass_on(values, axis, step):
    count = lax.axis_size(axis)
    pairs = [(i, i + step) for i in range(count) if 0 <= i + step < count]
    return lax.ppermute(values, axis, pairs)


def swap(values, axis, mask):
    return lax.ppermute(values, axis, [(i, i ^ mask) for i in range(lax.axis_size(axis))])


def gather_rows(values):
    count = lax.axis_size("fsdp")
    return jnp.concatenate([values] + [shift(values, "fsdp", k) for k in range(1, count)], 0)


def scatter_rows(low):
    count = lax.axis_size("fsdp")
    rows = low.shape[0] // count
    total = low[:rows].astype(F32)
    for k in range(1, count):
        total = total + shift(low[k * rows : (k + 1) * rows], "fsdp", -k).astype(F32)
    return total


def exchange(piece):
    count = lax.axis_size("fsdp")
    place = lax.axis_index("fsdp")
    return [piece(place)] + [shift(piece((place - k) % count), "fsdp", -k) for k in range(1, count)]


def in_order(pieces):
    count = len(pieces)
    stacked = jnp.stack(pieces + pieces[:-1])
    place = lax.axis_index("fsdp")
    return lax.dynamic_slice_in_dim(stacked, (count - place) % count, count, 0)


def stages():
    masks = []
    for axis, first in (("seq", 2), ("dp", 1)):
        mask = first
        while mask < lax.axis_size(axis):
            masks.append((axis, mask))
            mask *= 2
    return masks


def stage_bits():
    return [(lax.axis_index(axis) // mask) % 2 for axis, mask in stages()]


def quarter_count():
    return 2 ** len(stages())


def quarter_place():
    place = jnp.int32(0)
    for bit in stage_bits():
        place = place * 2 + bit
    return place


def core_place():
    return lax.axis_index("seq") % 2


def gather_quarters(values, flipped):
    chain = stages()
    order = list(range(len(chain)))
    order = order if flipped else order[::-1]
    held = []
    for at in order:
        axis, mask = chain[at]
        spot = sum(other < at for other in held)
        values = jnp.stack([values, swap(values, axis, mask)], spot)
        held.append(at)
    return values.reshape(quarter_count(), *values.shape[len(held) :])


def reduce_quarters(values, flipped, absolute):
    chain, bits = stages(), stage_bits()
    values = values.reshape(*([2] * len(chain)), *values.shape[1:])
    order = list(range(len(chain)))
    order = order[::-1] if flipped else order
    left = list(range(len(chain)))
    for at in order:
        axis, mask = chain[at]
        spot = left.index(at)
        left.remove(at)
        if absolute:
            keep = lax.dynamic_index_in_dim(values, bits[at], spot, False)
            send = lax.dynamic_index_in_dim(values, 1 - bits[at], spot, False)
        else:
            keep = lax.index_in_dim(values, 0, spot, False)
            send = lax.index_in_dim(values, 1, spot, False)
        values = (keep.astype(F32) + swap(send, axis, mask).astype(F32)).astype(BF)
    return values


def start_columns(weights):
    count = lax.axis_size("fsdp")
    rows = weights[0].shape[0] // quarter_count()
    core = core_place()
    own = [lax.dynamic_slice_in_dim(w, quarter_place() * rows, rows, 0) for w in weights]

    def piece(target):
        parts = []
        for w in own:
            width = w.shape[1] // (2 * count)
            parts.append(lax.dynamic_slice_in_dim(w, (2 * target + core) * width, width, 1))
        return jnp.concatenate(parts, 1)

    return in_order(exchange(piece))


def finish_columns(mine, flipped):
    whole = gather_quarters(mine, flipped)
    whole = whole.reshape(-1, whole.shape[-1])
    return whole, swap(whole, "seq", 1)


def start_grads(left, own, other, flipped):
    count = lax.axis_size("fsdp")
    arrived = swap(dot(left, other, 0, 0).astype(BF), "seq", 1)
    both = (dot(left, own, 0, 0) + arrived.astype(F32)).astype(BF)
    rows = both.shape[0] // (quarter_count() * count)
    return reduce_quarters(
        both.reshape(quarter_count(), count, rows, both.shape[1]), flipped, False
    )


def finish_grads(summed, widths, flipped):
    pieces = exchange(lambda target: lax.dynamic_index_in_dim(summed, target, 0, False))
    whole = gather_quarters(jnp.stack(pieces), flipped)
    return place_columns(whole, swap(whole, "seq", 1), widths)


def place_columns(own, other, widths):
    quarters, count, rows, _ = own.shape
    places = jnp.stack([quarter_place(), core_place(), lax.axis_index("fsdp")])

    def body(place_ref, own_ref, other_ref, *out_refs):
        first = place_ref[1] == 0
        start = 0
        for out_ref, width in zip(out_refs, widths):
            mine = own_ref[0, 0, :, start : start + width].astype(F32)
            theirs = other_ref[0, 0, :, start : start + width].astype(F32)
            out_ref[0, :, :width] = jnp.where(first, mine, theirs)
            out_ref[0, :, width:] = jnp.where(first, theirs, mine)
            start += width

    block = pl.BlockSpec((1, 1, rows, own.shape[3]), lambda q, z, place: (q, z, 0, 0))
    outs = pl.pallas_call(
        body,
        grid_spec=pltpu.PrefetchScalarGridSpec(
            num_scalar_prefetch=1,
            grid=(quarters, count),
            in_specs=[block, block],
            out_specs=[
                pl.BlockSpec(
                    (1, rows, 2 * width),
                    lambda q, z, place: (q ^ place[0], 0, lax.rem(z + place[2], count)),
                )
                for width in widths
            ],
        ),
        out_shape=[
            jax.ShapeDtypeStruct((quarters, rows, 2 * width * count), F32) for width in widths
        ],
        cost_estimate=pl.CostEstimate(flops=0, bytes_accessed=own.size * 12, transcendentals=0),
    )(places, own, other)
    return [out.reshape(quarters * rows, out.shape[2]) for out in outs]


def sum_rows(own, other, right, flipped):
    arrived = swap(dot(other, right, 0, 0).astype(BF), "seq", 1)
    both = (dot(own, right, 0, 0) + arrived.astype(F32)).astype(BF)
    rows = both.shape[0] // quarter_count()
    summed = reduce_quarters(both.reshape(quarter_count(), rows, both.shape[1]), flipped, True)
    whole = gather_quarters(summed, flipped)
    return place_rows(whole, swap(whole, "seq", 1))


def place_rows(own, other):
    quarters, rows, width = own.shape
    places = jnp.stack([quarter_place(), core_place()])

    def body(place_ref, own_ref, other_ref, out_ref):
        first = place_ref[1] == 0
        mine, theirs = own_ref[0].astype(F32), other_ref[0].astype(F32)
        out_ref[0, 0] = jnp.where(first, mine, theirs)
        out_ref[1, 0] = jnp.where(first, theirs, mine)

    half = width // 2
    block = pl.BlockSpec((1, rows, half), lambda q, c, place: (q, 0, c))
    out = pl.pallas_call(
        body,
        grid_spec=pltpu.PrefetchScalarGridSpec(
            num_scalar_prefetch=1,
            grid=(quarters, 2),
            in_specs=[block, block],
            out_specs=pl.BlockSpec(
                (2, 1, rows, half), lambda q, c, place: (0, q ^ place[0], 0, c)
            ),
        ),
        out_shape=jax.ShapeDtypeStruct((2, quarters, rows, width), F32),
        cost_estimate=pl.CostEstimate(flops=0, bytes_accessed=own.size * 12, transcendentals=0),
    )(places, own, other)
    return out.reshape(2 * quarters * rows, width)


def swap_quarters(pieces):
    bits = stage_bits()
    for at, bit in enumerate(bits):
        mask = 1 << (len(bits) - 1 - at)
        pieces = [jnp.where(bit == 1, pieces[c ^ mask], pieces[c]) for c in range(len(pieces))]
    return pieces


def spread(values):
    count, quarters = lax.axis_size("fsdp"), quarter_count()
    chunk = values.shape[1] // (count * quarters)
    groups = []
    for z in range(count):
        starts = [(z * quarters + q) * chunk for q in range(quarters)]
        groups.append(swap_quarters([values[:, s : s + chunk] for s in starts]))
    return jnp.concatenate([groups[z][q] for q in range(quarters) for z in range(count)], 1)


def unspread(values):
    count, quarters = lax.axis_size("fsdp"), quarter_count()
    chunk = values.shape[1] // (count * quarters)
    outs = []
    for z in range(count):
        starts = [(q * count + z) * chunk for q in range(quarters)]
        outs += swap_quarters([values[:, s : s + chunk] for s in starts])
    return jnp.concatenate(outs, 1)


def flip_state(states):
    if states.shape[0] % 2 == 0:
        half = states.shape[0] // 2
        return jnp.concatenate([states[half:], states[:half]], 0)
    half_k, half_v = states.shape[1] // 2, states.shape[2] // 2
    turned = jnp.concatenate([states[:, half_k:], states[:, :half_k]], 1)
    return jnp.concatenate([turned[:, :, half_v:], turned[:, :, :half_v]], 2)


def prefix_states(own, decay, sign):
    count = lax.axis_size("seq")
    low = own.astype(BF)
    flipped = flip_state(low)
    total = None
    for k in range(1, count):
        part = pass_on(flipped if k % 2 else low, "seq", sign * k).astype(F32)
        if k > 1:
            part = part * decay ** (k - 1)
        total = part if total is None else total + part
    return total


def sum_everywhere(values):
    for axis in ("seq", "fsdp", "dp"):
        mask = 1
        while mask < lax.axis_size(axis):
            values = values + swap(values, axis, mask)
            mask *= 2
    return values


def on_device(
    tokens,
    mixer_gain,
    mixer_shift,
    w_query,
    w_key,
    w_value,
    w_gate,
    decay_exponent,
    group_gain,
    group_shift,
    w_out,
    feed_gain,
    feed_shift,
    w_act,
    w_lin,
    w_down,
    cotangent,
):
    count = lax.axis_size("fsdp")
    place = lax.axis_index("fsdp")
    core = core_place()
    rows = tokens.shape[0]
    group = rows * count
    spans = group // SPAN
    local_heads = H // count
    q_set, v_set = local_heads * KD // 2, local_heads * VD // 2
    h_set = w_act.shape[1] // (2 * count)
    key_scale = KD ** (-0.5)

    def natural(values):
        if spans == 1:
            return values
        blocks = values.reshape(count, rows, values.shape[1])
        pieces = [blocks[0]] + [blocks[count - k] for k in range(1, count)]
        return in_order(pieces).reshape(values.shape)

    def relative(values):
        if spans == 1:
            return values
        blocks = values.reshape(count, rows, values.shape[1])
        doubled = jnp.concatenate([blocks, blocks[:-1]])
        turned = lax.dynamic_slice_in_dim(doubled, place, count, 0)
        return jnp.stack([turned[0]] + [turned[count - k] for k in range(1, count)]).reshape(
            values.shape
        )

    def own_rows(weight):
        half = weight.shape[0] // 2
        return jnp.concatenate(
            [lax.dynamic_slice_in_dim(weight, (core ^ j) * half, half, 0) for j in (0, 1)], 0
        )

    def heads_of(pair, width):
        if local_heads % 2:
            return [natural(jnp.concatenate(pair, 1))]
        return [
            natural(part)[:, i * width : (i + 1) * width]
            for part in pair
            for i in range(local_heads // 2)
        ]

    def pair_of(heads):
        if local_heads % 2:
            half = heads[0].shape[1] // 2
            return relative(heads[0][:, :half]), relative(heads[0][:, half:])
        half = len(heads) // 2
        return tuple(
            relative(jnp.concatenate(heads[j * half : (j + 1) * half], 1)) for j in (0, 1)
        )

    if local_heads % 2:
        head_places = [place]
    else:
        half_heads = local_heads // 2
        head_places = [
            place * local_heads + (core ^ j) * half_heads + i
            for j in (0, 1)
            for i in range(half_heads)
        ]

    inputs = tokens.astype(F32)
    key_value_start = start_columns((w_key, w_value))
    query_gate_start = start_columns((w_query, w_gate))
    scaled_in, inverse_in = norm_parts(inputs)
    normed_own = spread((scaled_in * mixer_gain + mixer_shift).astype(BF))
    normed = gather_rows(after(normed_own, key_value_start, query_gate_start))
    key_value = finish_columns(key_value_start, False)
    query_gate = finish_columns(query_gate_start, True)
    free_act, free_lin = lax.optimization_barrier((w_act, w_lin, normed))[:2]
    act_start = start_columns((free_act,))
    lin_start = start_columns((free_lin,))
    act_set = finish_columns(act_start, False)
    lin_set = finish_columns(lin_start, True)
    upstream = gather_rows(after(cotangent, act_start, lin_start))
    out_rel, down_rel = own_rows(w_out), own_rows(w_down)

    log_rates = jnp.log1p(-jnp.exp2(-decay_exponent.astype(F32)))
    if spans == 1:
        index = jnp.arange(SPAN)
        positions = ((place - index // rows) % count * rows + index % rows).astype(F32)
    else:
        positions = jnp.arange(SPAN).astype(F32)
    offsets = positions[:, None] - positions[None, :]
    tables = []
    for at in head_places:
        log_rate = lax.dynamic_index_in_dim(log_rates, at, 0, False)
        inside = (
            jnp.where(offsets >= 0, jnp.exp(jnp.maximum(offsets, 0.0) * log_rate), 0.0) * key_scale
        )
        tables.append(
            (
                inside,
                key_scale * jnp.exp((positions + 1.0) * log_rate)[:, None],
                jnp.exp((SPAN - 1.0 - positions) * log_rate)[:, None],
                jnp.exp(SPAN * log_rate),
            )
        )
    decays = jnp.stack([table[3] for table in tables])[:, None, None]

    kv_pair = [dot(normed, part, 1, 0) for part in key_value]
    keys = heads_of([part[:, :q_set].astype(BF) for part in kv_pair], KD)
    values = heads_of([part[:, q_set:].astype(BF) for part in kv_pair], VD)

    def cut(array, block):
        return array[block * SPAN : (block + 1) * SPAN]

    local_states, finals = [], []
    for head in range(local_heads):
        _, _, key_factor, carry = tables[head]
        state, states = None, []
        for block in range(spans):
            scaled_keys = (cut(keys[head], block).astype(F32) * key_factor).astype(BF)
            update = dot(scaled_keys, cut(values[head], block), 0, 0)
            states.append(state)
            state = update if state is None else state * carry + update
        local_states.append(states)
        finals.append(state)
    entering = prefix_states(jnp.stack(finals), decays**spans, 1)

    qg_pair = [dot(normed, part, 1, 0) for part in query_gate]
    queries = heads_of([part[:, :q_set].astype(BF) for part in qg_pair], KD)
    gate_pre = [part[:, q_set:] for part in qg_pair]

    masked_all, state_all, normal_all, inv_all = [], [], [], []
    for head in range(local_heads):
        inside, query_factor, _, carry = tables[head]
        for block in range(spans):
            query = cut(queries[head], block)
            masked = (dot(query, cut(keys[head], block), 1, 1) * inside).astype(BF)
            state = entering[head] * carry**block
            if local_states[head][block] is not None:
                state = state + local_states[head][block]
            state_low = state.astype(BF)
            mixed = dot(masked, cut(values[head], block), 1, 0) + query_factor * dot(
                query, state_low, 1, 0
            )
            mean = jnp.mean(mixed, -1, keepdims=True)
            inv_std = lax.rsqrt(jnp.mean(mixed * mixed, -1, keepdims=True) - mean * mean + EPSILON)
            masked_all.append(masked)
            state_all.append(state_low)
            normal_all.append((mixed - mean) * inv_std)
            inv_all.append(inv_std)

    def join(parts):
        return pair_of(
            [
                jnp.concatenate(parts[head * spans : (head + 1) * spans], 0)
                for head in range(local_heads)
            ]
        )

    headed = join([normal.astype(BF) for normal in normal_all])
    gains, biases = [], []
    for j in (0, 1):
        start = (2 * place + (core ^ j)) * v_set
        gains.append(lax.dynamic_slice_in_dim(group_gain, start, v_set, 0))
        biases.append(lax.dynamic_slice_in_dim(group_shift, start, v_set, 0))
    silus = [gate * jax.nn.sigmoid(gate) for gate in gate_pre]
    gated = jnp.concatenate(
        [
            (silus[j] * (headed[j].astype(F32) * gains[j] + biases[j])).astype(BF)
            for j in (0, 1)
        ],
        1,
    )

    middle = inputs + scatter_rows(dot(gated, out_rel, 1, 0).astype(BF))
    scaled_mid, inverse_mid = norm_parts(middle)
    second = gather_rows(spread((scaled_mid * feed_gain + feed_shift).astype(BF)))
    hidden_grad = dot(upstream, down_rel, 1, 1)
    hidden, act_low, lin_low = [], [], []
    for j in (0, 1):
        active, linear = dot(second, act_set[j], 1, 0), dot(second, lin_set[j], 1, 0)
        upper = hidden_grad[:, j * h_set : (j + 1) * h_set]
        cdf = 0.5 * (1.0 + lax.erf(active * (2.0**-0.5)))
        gelu = active * cdf
        slope = cdf + active * jnp.exp(-0.5 * active * active) * (0.5 / jnp.pi) ** 0.5
        hidden.append((gelu * linear).astype(BF))
        act_low.append((upper * linear * slope).astype(BF))
        lin_low.append((upper * gelu).astype(BF))
    second_partial = (
        dot(act_low[0], act_set[0], 1, 1)
        + dot(act_low[1], act_set[1], 1, 1)
        + dot(lin_low[0], lin_set[0], 1, 1)
        + dot(lin_low[1], lin_set[1], 1, 1)
    ).astype(BF)
    second_grad = unspread(scatter_rows(second_partial))

    grad_down = sum_rows(hidden[0], hidden[1], upstream, False)
    act_sum = start_grads(second, act_low[0], act_low[1], False)
    lin_sum = start_grads(second, lin_low[0], lin_low[1], True)

    mid_term, grad_feed_gain, grad_feed_shift = norm_pull(
        scaled_mid, inverse_mid, feed_gain, second_grad
    )
    middle_grad = cotangent.astype(F32) + mid_term
    branch = gather_rows(middle_grad.astype(BF))
    (grad_act,) = finish_grads(after(act_sum, branch), (h_set,), False)
    (grad_lin,) = finish_grads(after(lin_sum, branch), (h_set,), True)
    down_partial = dot(jnp.concatenate(hidden, 1), down_rel, 1, 0).astype(BF)
    result = (middle + scatter_rows(after(down_partial, branch))).astype(BF)

    gated_grad = dot(branch, out_rel, 1, 1)
    gate_low, group_sums, headed_low = [], [], []
    for j in (0, 1):
        upper = gated_grad[:, j * v_set : (j + 1) * v_set]
        sigmoid = jax.nn.sigmoid(gate_pre[j])
        wide = headed[j].astype(F32)
        gate_low.append(
            (
                upper
                * (wide * gains[j] + biases[j])
                * (sigmoid * (1.0 + gate_pre[j] * (1.0 - sigmoid)))
            ).astype(BF)
        )
        shift_terms = upper * (gate_pre[j] * sigmoid)
        group_sums.append((jnp.sum(shift_terms * wide, 0), jnp.sum(shift_terms, 0)))
        headed_low.append((shift_terms * gains[j]).astype(BF))
    headed_grad = heads_of(headed_low, VD)
    grad_out = sum_rows(gated[:, :v_set], gated[:, v_set:], branch, True)

    mixed_grads, terms = [], []
    for head in range(local_heads):
        _, query_factor, _, carry = tables[head]
        carried, later = None, [None] * spans
        for block in range(spans):
            at = head * spans + block
            upper = cut(headed_grad[head], block).astype(F32)
            normal = normal_all[at]
            mixed_grads.append(
                (
                    inv_all[at]
                    * (
                        upper
                        - jnp.mean(upper, -1, keepdims=True)
                        - normal * jnp.mean(upper * normal, -1, keepdims=True)
                    )
                ).astype(BF)
            )
        for block in reversed(range(spans)):
            later[block] = carried
            scaled_query = (cut(queries[head], block).astype(F32) * query_factor).astype(BF)
            term = dot(scaled_query, mixed_grads[head * spans + block], 0, 0)
            carried = term if carried is None else carried * carry + term
        terms.append((later, carried))
    leaving = prefix_states(jnp.stack([term[1] for term in terms]), decays**spans, -1)

    query_grads, key_grads, value_grads = [], [], []
    for head in range(local_heads):
        inside, query_factor, key_factor, carry = tables[head]
        for block in range(spans):
            at = head * spans + block
            query, key, value = (cut(array[head], block) for array in (queries, keys, values))
            carried = leaving[head] * carry ** (spans - 1 - block)
            if terms[head][0][block] is not None:
                carried = carried + terms[head][0][block]
            carried_low = carried.astype(BF)
            score_grad = (dot(mixed_grads[at], value, 1, 1) * inside).astype(BF)
            query_grads.append(
                (
                    dot(score_grad, key, 1, 0)
                    + query_factor * dot(mixed_grads[at], state_all[at], 1, 1)
                ).astype(BF)
            )
            key_grads.append(
                (
                    dot(score_grad, query, 0, 0) + key_factor * dot(value, carried_low, 1, 1)
                ).astype(BF)
            )
            value_grads.append(
                (
                    dot(masked_all[at], mixed_grads[at], 0, 0)
                    + key_factor * dot(key, carried_low, 1, 0)
                ).astype(BF)
            )
    query_low, key_low, value_low = join(query_grads), join(key_grads), join(value_grads)
    kv_low = [jnp.concatenate([key_low[j], value_low[j]], 1) for j in (0, 1)]
    qg_low = [jnp.concatenate([query_low[j], gate_low[j]], 1) for j in (0, 1)]
    normed_partial = (
        dot(kv_low[0], key_value[0], 1, 1)
        + dot(kv_low[1], key_value[1], 1, 1)
        + dot(qg_low[0], query_gate[0], 1, 1)
        + dot(qg_low[1], query_gate[1], 1, 1)
    ).astype(BF)
    normed_grad = unspread(scatter_rows(normed_partial))
    kv_sum = start_grads(normed, kv_low[0], kv_low[1], False)
    qg_sum = start_grads(normed, qg_low[0], qg_low[1], True)
    grad_key, grad_value = finish_grads(kv_sum, (q_set, v_set), False)
    grad_query, grad_gate = finish_grads(qg_sum, (q_set, v_set), True)
    in_term, grad_mixer_gain, grad_mixer_shift = norm_pull(
        scaled_in, inverse_in, mixer_gain, normed_grad
    )
    grad_tokens = (middle_grad + in_term).astype(BF)

    def placed(parts):
        out = jnp.zeros(group_gain.shape, F32)
        for j in (0, 1):
            out = lax.dynamic_update_slice_in_dim(
                out, parts[j], (2 * place + (core ^ j)) * v_set, 0
            )
        return out

    def total(parts):
        sizes = [part.shape[0] for part in parts]
        packed = sum_everywhere(jnp.concatenate(parts).reshape(-1, 128)).reshape(-1)
        outs, start = [], 0
        for size in sizes:
            outs.append(packed[start : start + size])
            start += size
        return outs

    grad_group_gain, grad_group_shift, grad_feed_gain, grad_feed_shift = total(
        [
            placed([sums[0] for sums in group_sums]),
            placed([sums[1] for sums in group_sums]),
            grad_feed_gain,
            grad_feed_shift,
        ]
    )
    grad_mixer_gain, grad_mixer_shift = total([grad_mixer_gain, grad_mixer_shift])
    return (
        result,
        grad_tokens,
        grad_query,
        grad_key,
        grad_value,
        grad_gate,
        grad_out,
        grad_act,
        grad_lin,
        grad_down,
        grad_mixer_gain,
        grad_mixer_shift,
        grad_group_gain,
        grad_group_shift,
        grad_feed_gain,
        grad_feed_shift,
    )


def solution(mesh):
    rows = P(("dp", "seq", "fsdp"), None)
    shard = P("fsdp", None)
    return jax.shard_map(
        on_device,
        mesh=mesh,
        in_specs=(rows, P(), P())
        + (shard,) * 4
        + (P(), P(), P(), shard, P(), P())
        + (shard,) * 3
        + (rows,),
        out_specs=(rows, rows) + (shard,) * 8 + (P(),) * 6,
        check_vma=False,
    )
```

```python
import jax
import jax.numpy as jnp
from jax import lax
from jax.experimental import pallas as pl
from jax.experimental.pallas import tpu as pltpu
from jax.sharding import PartitionSpec as P

H = 8
KD = 256
VD = 512
SPAN = 512
EPSILON = 1e-05
BF = jnp.bfloat16
F32 = jnp.float32


def norm_parts(values):
    center = values - jnp.mean(values, -1, keepdims=True)
    inverse = lax.rsqrt(jnp.mean(center * center, -1, keepdims=True) + EPSILON)
    return center * inverse, inverse


def norm_pull(scaled, inverse, gain, grad):
    lifted = grad * gain
    term = inverse * (
        lifted
        - jnp.mean(lifted, -1, keepdims=True)
        - scaled * jnp.mean(lifted * scaled, -1, keepdims=True)
    )
    return term, jnp.sum(grad * scaled, 0), jnp.sum(grad, 0)


def dot(left, right, left_axis, right_axis):
    return lax.dot_general(
        left, right, (((left_axis,), (right_axis,)), ((), ())), preferred_element_type=F32
    )


def after(values, *others):
    return lax.optimization_barrier((values, *others))[0]


def shift(values, axis, step):
    count = lax.axis_size(axis)
    return lax.ppermute(values, axis, [(i, (i + step) % count) for i in range(count)])


def pass_on(values, axis, step):
    count = lax.axis_size(axis)
    pairs = [(i, i + step) for i in range(count) if 0 <= i + step < count]
    return lax.ppermute(values, axis, pairs)


def swap(values, axis, mask):
    return lax.ppermute(values, axis, [(i, i ^ mask) for i in range(lax.axis_size(axis))])


def tie(*trees):
    return lax.optimization_barrier(trees)


def slot_offsets():
    count = lax.axis_size("fsdp")
    return [0, -1, 1, 2] if count == 4 else [0] + [-k for k in range(1, count)]


def gather_start(values):
    count = lax.axis_size("fsdp")
    if count == 4:
        return [values, pass_on(values, "fsdp", 1), pass_on(values, "fsdp", -1)]
    return [values] + [shift(values, "fsdp", k) for k in range(1, count)]


def gather_rest(parts):
    if lax.axis_size("fsdp") != 4:
        return parts
    place = lax.axis_index("fsdp")
    own, below, above = parts
    far_down = lax.ppermute(above, "fsdp", [(1, 0), (2, 1)])
    far_up = lax.ppermute(below, "fsdp", [(1, 2), (2, 3)])
    ends = lax.ppermute(jnp.where(place == 2, above, below), "fsdp", [(2, 0), (1, 3)])
    return [own, below, above, far_down, far_up, ends]


def gather_join(parts):
    if lax.axis_size("fsdp") != 4:
        return jnp.concatenate(parts, 0)
    place = lax.axis_index("fsdp")
    own, below, above, far_down, far_up, ends = parts
    return jnp.concatenate(
        [
            own,
            jnp.where(place == 0, ends, below),
            jnp.where(place == 3, ends, above),
            jnp.where(place < 2, far_down, far_up),
        ],
        0,
    )


def gather_rows(values):
    return gather_join(gather_rest(gather_start(values)))


def scatter_rows(low):
    count = lax.axis_size("fsdp")
    rows = low.shape[0] // count
    parts = [low[k * rows : (k + 1) * rows] for k in range(count)]
    if count != 4:
        total = parts[0].astype(F32)
        for k in range(1, count):
            total = total + shift(parts[k], "fsdp", -k).astype(F32)
        return total
    place = lax.axis_index("fsdp")
    own, below, above, far = parts
    from_below = lax.ppermute(far, "fsdp", [(0, 1), (1, 2)])
    from_above = lax.ppermute(far, "fsdp", [(2, 1), (3, 2)])
    ends = lax.ppermute(jnp.where(place == 0, below, above), "fsdp", [(0, 2), (3, 1)])
    ends = ends.astype(F32)
    up = above.astype(F32) + from_below.astype(F32) + jnp.where(place == 2, ends, 0.0)
    down = below.astype(F32) + from_above.astype(F32) + jnp.where(place == 1, ends, 0.0)
    return (
        own.astype(F32)
        + pass_on(up.astype(BF), "fsdp", 1).astype(F32)
        + pass_on(down.astype(BF), "fsdp", -1).astype(F32)
    )


def exchange(piece):
    count = lax.axis_size("fsdp")
    place = lax.axis_index("fsdp")
    return [piece(place)] + [shift(piece((place - k) % count), "fsdp", -k) for k in range(1, count)]


def in_order(pieces):
    count = len(pieces)
    stacked = jnp.stack(pieces + pieces[:-1])
    place = lax.axis_index("fsdp")
    return lax.dynamic_slice_in_dim(stacked, (count - place) % count, count, 0)


def stages():
    masks = []
    for axis, first in (("seq", 2), ("dp", 1)):
        mask = first
        while mask < lax.axis_size(axis):
            masks.append((axis, mask))
            mask *= 2
    return masks


def stage_bits():
    return [(lax.axis_index(axis) // mask) % 2 for axis, mask in stages()]


def quarter_count():
    return 2 ** len(stages())


def quarter_place():
    place = jnp.int32(0)
    for bit in stage_bits():
        place = place * 2 + bit
    return place


def core_place():
    return lax.axis_index("seq") % 2


class Task:
    def __init__(self, values, steps):
        self.values, self.steps = values, list(steps)

    def step(self, times=1):
        for _ in range(times):
            self.values = self.steps.pop(0)(self.values)

    def finish(self):
        self.step(len(self.steps))
        return self.values


def sync(tasks, *trees):
    values, trees = lax.optimization_barrier(([task.values for task in tasks], trees))
    for task, held in zip(tasks, values):
        task.values = held
    return trees


def gather_steps(flipped, ready):
    chain = stages()
    order = list(range(len(chain)))
    order = order if flipped else order[::-1]
    held = []

    def send(at):
        def run(values):
            axis, mask = chain[at]
            return [values, swap(values, axis, mask), at]

        return run

    def join(values):
        mine, arrived, at = values
        spot = sum(other < at for other in held)
        held.append(at)
        return jnp.stack([mine, arrived], spot)

    def first(values):
        return send(order[0])(ready(values))[:2]

    def second(values):
        now = join([*values, order[0]])
        for at in order[1:-1]:
            now = join(send(at)(now))
        return send(order[-1])(now)[:2]

    def third(values):
        now = join([*values, order[-1]])
        now = now.reshape(quarter_count(), *now.shape[len(held) :])
        return [now, swap(now, "seq", 1)]

    return [first, second, third]


def reduce_steps(own_part, flipped, absolute):
    chain = stages()
    order = list(range(len(chain)))
    order = order[::-1] if flipped else order
    left = list(range(len(chain)))

    def split(values, at):
        axis, mask = chain[at]
        spot = left.index(at)
        left.remove(at)
        if absolute:
            bit = (lax.axis_index(axis) // mask) % 2
            keep = lax.dynamic_index_in_dim(values, bit, spot, False)
            send = lax.dynamic_index_in_dim(values, 1 - bit, spot, False)
        else:
            keep = lax.index_in_dim(values, 0, spot, False)
            send = lax.index_in_dim(values, 1, spot, False)
        return [keep, swap(send, axis, mask)]

    def add(values):
        return (values[0].astype(F32) + values[1].astype(F32)).astype(BF)

    def core(values):
        return [swap(values[0], "seq", 1)]

    def first(values):
        both = (own_part() + values[0].astype(F32)).astype(BF)
        count = lax.axis_size("fsdp")
        if absolute:
            tail = (both.shape[0] // quarter_count(), both.shape[1])
        else:
            tail = (count, both.shape[0] // (quarter_count() * count), both.shape[1])
        return split(both.reshape(*([2] * len(chain)), *tail), order[0])

    def second(values):
        now = add(values)
        for at in order[1:-1]:
            now = add(split(now, at))
        return split(now, order[-1])

    return [core, first, second], add


def weight_task(weights, flipped):
    count = lax.axis_size("fsdp")
    rows = weights[0].shape[0] // quarter_count()
    core = core_place()
    own = [lax.dynamic_slice_in_dim(w, quarter_place() * rows, rows, 0) for w in weights]

    def piece(target):
        parts = []
        for w in own:
            width = w.shape[1] // (2 * count)
            parts.append(lax.dynamic_slice_in_dim(w, (2 * target + core) * width, width, 1))
        return jnp.concatenate(parts, 1)

    return Task(exchange(piece), gather_steps(flipped, in_order))


def pair_of_weights(task):
    return [part.reshape(-1, part.shape[-1]) for part in task.values]


def column_grads(left, own, other, widths, flipped):
    steps, add = reduce_steps(lambda: dot(left, own, 0, 0), flipped, False)

    def across(values):
        summed = add(values)
        return exchange(lambda target: lax.dynamic_index_in_dim(summed, target, 0, False))

    def out(values):
        return place_columns(values[0], values[1], widths)

    return Task(
        [dot(left, other, 0, 0).astype(BF)],
        [*steps, across, *gather_steps(flipped, jnp.stack), out],
    )


def row_grads(own, other, right, flipped):
    steps, add = reduce_steps(lambda: dot(own, right, 0, 0), flipped, True)

    def out(values):
        return [place_rows(values[0], values[1])]

    return Task(
        [dot(other, right, 0, 0).astype(BF)],
        [*steps, *gather_steps(flipped, add), out],
    )


def place_columns(own, other, widths):
    quarters, count, rows, _ = own.shape
    places = jnp.stack([quarter_place(), core_place(), lax.axis_index("fsdp")])

    def body(place_ref, own_ref, other_ref, *out_refs):
        first = place_ref[1] == 0
        start = 0
        for out_ref, width in zip(out_refs, widths):
            spot = slice(start, start + width)

            @pl.when(first)
            def _():
                out_ref[0, :, :width] = own_ref[0, 0, :, spot].astype(F32)
                out_ref[0, :, width:] = other_ref[0, 0, :, spot].astype(F32)

            @pl.when(jnp.logical_not(first))
            def _():
                out_ref[0, :, :width] = other_ref[0, 0, :, spot].astype(F32)
                out_ref[0, :, width:] = own_ref[0, 0, :, spot].astype(F32)

            start += width

    block = pl.BlockSpec((1, 1, rows, own.shape[3]), lambda q, z, place: (q, z, 0, 0))
    outs = pl.pallas_call(
        body,
        grid_spec=pltpu.PrefetchScalarGridSpec(
            num_scalar_prefetch=1,
            grid=(quarters, count),
            in_specs=[block, block],
            out_specs=[
                pl.BlockSpec(
                    (1, rows, 2 * width),
                    lambda q, z, place: (q ^ place[0], 0, lax.rem(z + place[2], count)),
                )
                for width in widths
            ],
        ),
        out_shape=[
            jax.ShapeDtypeStruct((quarters, rows, 2 * width * count), F32) for width in widths
        ],
        cost_estimate=pl.CostEstimate(flops=0, bytes_accessed=own.size * 12, transcendentals=0),
    )(places, own, other)
    return [out.reshape(quarters * rows, out.shape[2]) for out in outs]


def place_rows(own, other):
    quarters, rows, width = own.shape
    places = jnp.stack([quarter_place(), core_place()])

    def body(place_ref, own_ref, other_ref, out_ref):
        first = place_ref[1] == 0

        @pl.when(first)
        def _():
            out_ref[0, 0] = own_ref[0].astype(F32)
            out_ref[1, 0] = other_ref[0].astype(F32)

        @pl.when(jnp.logical_not(first))
        def _():
            out_ref[0, 0] = other_ref[0].astype(F32)
            out_ref[1, 0] = own_ref[0].astype(F32)

    half = width // 2
    block = pl.BlockSpec((1, rows, half), lambda q, c, place: (q, 0, c))
    out = pl.pallas_call(
        body,
        grid_spec=pltpu.PrefetchScalarGridSpec(
            num_scalar_prefetch=1,
            grid=(quarters, 2),
            in_specs=[block, block],
            out_specs=pl.BlockSpec(
                (2, 1, rows, half), lambda q, c, place: (0, q ^ place[0], 0, c)
            ),
        ),
        out_shape=jax.ShapeDtypeStruct((2, quarters, rows, width), F32),
        cost_estimate=pl.CostEstimate(flops=0, bytes_accessed=own.size * 12, transcendentals=0),
    )(places, own, other)
    return out.reshape(2 * quarters * rows, width)


def swap_quarters(pieces):
    bits = stage_bits()
    for at, bit in enumerate(bits):
        mask = 1 << (len(bits) - 1 - at)
        pieces = [jnp.where(bit == 1, pieces[c ^ mask], pieces[c]) for c in range(len(pieces))]
    return pieces


def spread(values):
    count, quarters = lax.axis_size("fsdp"), quarter_count()
    chunk = values.shape[1] // (count * quarters)
    groups = []
    for z in range(count):
        starts = [(z * quarters + q) * chunk for q in range(quarters)]
        groups.append(swap_quarters([values[:, s : s + chunk] for s in starts]))
    return jnp.concatenate([groups[z][q] for q in range(quarters) for z in range(count)], 1)


def unspread(values):
    count, quarters = lax.axis_size("fsdp"), quarter_count()
    chunk = values.shape[1] // (count * quarters)
    outs = []
    for z in range(count):
        starts = [(q * count + z) * chunk for q in range(quarters)]
        outs += swap_quarters([values[:, s : s + chunk] for s in starts])
    return jnp.concatenate(outs, 1)


def flip_state(states):
    if states.shape[0] % 2 == 0:
        half = states.shape[0] // 2
        return jnp.concatenate([states[half:], states[:half]], 0)
    half_k, half_v = states.shape[1] // 2, states.shape[2] // 2
    turned = jnp.concatenate([states[:, half_k:], states[:, :half_k]], 1)
    return jnp.concatenate([turned[:, :, half_v:], turned[:, :, :half_v]], 2)


def state_start(own, sign):
    count = lax.axis_size("seq")
    low = own.astype(BF)
    flipped = flip_state(low)
    return [pass_on(flipped if k % 2 else low, "seq", sign * k) for k in range(1, count)]


def state_join(parts, decay):
    total = parts[0].astype(F32)
    for k, part in enumerate(parts[1:], 1):
        total = total + part.astype(F32) * decay**k
    return total


def sum_everywhere(values):
    for axis in ("seq", "fsdp", "dp"):
        mask = 1
        while mask < lax.axis_size(axis):
            values = values + swap(values, axis, mask)
            mask *= 2
    return values


def on_device(
    tokens,
    mixer_gain,
    mixer_shift,
    w_query,
    w_key,
    w_value,
    w_gate,
    decay_exponent,
    group_gain,
    group_shift,
    w_out,
    feed_gain,
    feed_shift,
    w_act,
    w_lin,
    w_down,
    cotangent,
):
    count = lax.axis_size("fsdp")
    place = lax.axis_index("fsdp")
    core = core_place()
    rows = tokens.shape[0]
    group = rows * count
    spans = group // SPAN
    local_heads = H // count
    q_set, v_set = local_heads * KD // 2, local_heads * VD // 2
    h_set = w_act.shape[1] // (2 * count)
    key_scale = KD ** (-0.5)

    def natural(values):
        if spans == 1:
            return values
        blocks = values.reshape(count, rows, values.shape[1])
        pieces = [blocks[0]] + [blocks[count - k] for k in range(1, count)]
        return in_order(pieces).reshape(values.shape)

    def relative(values):
        if spans == 1:
            return values
        blocks = values.reshape(count, rows, values.shape[1])
        doubled = jnp.concatenate([blocks, blocks[:-1]])
        turned = lax.dynamic_slice_in_dim(doubled, place, count, 0)
        return jnp.stack([turned[0]] + [turned[count - k] for k in range(1, count)]).reshape(
            values.shape
        )

    def own_rows(weight):
        half = weight.shape[0] // 2
        return jnp.concatenate(
            [lax.dynamic_slice_in_dim(weight, (core ^ j) * half, half, 0) for j in (0, 1)], 0
        )

    def heads_of(pair, width):
        if local_heads % 2:
            return [natural(jnp.concatenate(pair, 1))]
        return [
            natural(part)[:, i * width : (i + 1) * width]
            for part in pair
            for i in range(local_heads // 2)
        ]

    def pair_of(heads):
        if local_heads % 2:
            half = heads[0].shape[1] // 2
            return relative(heads[0][:, :half]), relative(heads[0][:, half:])
        half = len(heads) // 2
        return tuple(
            relative(jnp.concatenate(heads[j * half : (j + 1) * half], 1)) for j in (0, 1)
        )

    if local_heads % 2:
        head_places = [place]
    else:
        half_heads = local_heads // 2
        head_places = [
            place * local_heads + (core ^ j) * half_heads + i
            for j in (0, 1)
            for i in range(half_heads)
        ]

    inputs = tokens.astype(F32)
    value_task = weight_task((w_value,), False)
    query_key_task = weight_task((w_query, w_key), True)
    scaled_in, inverse_in = norm_parts(inputs)
    normed_own = spread((scaled_in * mixer_gain + mixer_shift).astype(BF))
    first_tasks = [value_task, query_key_task]
    normed_own, free_gate = sync(first_tasks, normed_own, w_gate)
    gate_task = weight_task((free_gate,), True)
    for task in first_tasks:
        task.step()
    (normed_own,) = sync([*first_tasks, gate_task], normed_own)
    for task in first_tasks:
        task.step()
    normed_parts = gather_start(normed_own)
    (normed_parts,) = tie(normed_parts)
    normed_parts = gather_rest(normed_parts)
    sync(first_tasks)
    (gate_values,) = tie(gate_task.values)
    for task in first_tasks:
        task.step()
    gate_task.step()
    normed_parts, late = sync([gate_task], normed_parts, (cotangent, w_act, w_lin))
    normed = gather_join(normed_parts)
    value_set, query_key_set = pair_of_weights(value_task), pair_of_weights(query_key_task)
    gate_task.step()
    upstream_parts = gather_start(late[0])
    out_rel, down_rel = own_rows(w_out), own_rows(w_down)

    log_rates = jnp.log1p(-jnp.exp2(-decay_exponent.astype(F32)))
    if spans == 1:
        index = jnp.arange(SPAN)
        steps = jnp.zeros(SPAN, jnp.int32)
        for slot, offset in enumerate(slot_offsets()):
            steps = jnp.where(index // rows == slot, offset, steps)
        positions = ((place + steps + count) % count * rows + index % rows).astype(F32)
    else:
        positions = jnp.arange(SPAN).astype(F32)
    offsets = positions[:, None] - positions[None, :]
    tables = []
    for at in head_places:
        log_rate = lax.dynamic_index_in_dim(log_rates, at, 0, False)
        inside = (
            jnp.where(offsets >= 0, jnp.exp(jnp.maximum(offsets, 0.0) * log_rate), 0.0) * key_scale
        )
        tables.append(
            (
                inside,
                key_scale * jnp.exp((positions + 1.0) * log_rate)[:, None],
                jnp.exp((SPAN - 1.0 - positions) * log_rate)[:, None],
                jnp.exp(SPAN * log_rate),
            )
        )
    decays = jnp.stack([table[3] for table in tables])[:, None, None]

    value_pair = [dot(normed, part, 1, 0).astype(BF) for part in value_set]
    query_key_pair = [dot(normed, part, 1, 0).astype(BF) for part in query_key_set]
    keys = heads_of([part[:, q_set:] for part in query_key_pair], KD)
    values = heads_of(value_pair, VD)
    queries = heads_of([part[:, :q_set] for part in query_key_pair], KD)

    def cut(array, block):
        return array[block * SPAN : (block + 1) * SPAN]

    local_states, finals = [], []
    for head in range(local_heads):
        _, _, key_factor, carry = tables[head]
        state, states = None, []
        for block in range(spans):
            scaled_keys = (cut(keys[head], block).astype(F32) * key_factor).astype(BF)
            update = dot(scaled_keys, cut(values[head], block), 0, 0)
            states.append(state)
            state = update if state is None else state * carry + update
        local_states.append(states)
        finals.append(state)
    entering_parts = state_start(jnp.stack(finals), 1)
    (upstream_parts,) = tie(upstream_parts)
    upstream_parts = gather_rest(upstream_parts)
    entering_parts, late = sync([gate_task], entering_parts, late)
    entering = state_join(entering_parts, decays**spans)
    gate_task.step()
    gate_set = pair_of_weights(gate_task)
    gate_pre = [dot(normed, part, 1, 0) for part in gate_set]
    act_task, lin_task = weight_task((late[1],), False), weight_task((late[2],), True)
    feed_tasks = [act_task, lin_task]

    masked_all, state_all, normal_all, inv_all = [], [], [], []
    for head in range(local_heads):
        inside, query_factor, _, carry = tables[head]
        for block in range(spans):
            query = cut(queries[head], block)
            masked = (dot(query, cut(keys[head], block), 1, 1) * inside).astype(BF)
            state = entering[head] * carry**block
            if local_states[head][block] is not None:
                state = state + local_states[head][block]
            state_low = state.astype(BF)
            mixed = dot(masked, cut(values[head], block), 1, 0) + query_factor * dot(
                query, state_low, 1, 0
            )
            mean = jnp.mean(mixed, -1, keepdims=True)
            inv_std = lax.rsqrt(jnp.mean(mixed * mixed, -1, keepdims=True) - mean * mean + EPSILON)
            masked_all.append(masked)
            state_all.append(state_low)
            normal_all.append((mixed - mean) * inv_std)
            inv_all.append(inv_std)

    def join(parts):
        return pair_of(
            [
                jnp.concatenate(parts[head * spans : (head + 1) * spans], 0)
                for head in range(local_heads)
            ]
        )

    headed = join([normal.astype(BF) for normal in normal_all])
    gains, biases = [], []
    for j in (0, 1):
        start = (2 * place + (core ^ j)) * v_set
        gains.append(lax.dynamic_slice_in_dim(group_gain, start, v_set, 0))
        biases.append(lax.dynamic_slice_in_dim(group_shift, start, v_set, 0))
    silus = [gate * jax.nn.sigmoid(gate) for gate in gate_pre]
    gated = jnp.concatenate(
        [
            (silus[j] * (headed[j].astype(F32) * gains[j] + biases[j])).astype(BF)
            for j in (0, 1)
        ],
        1,
    )

    sync(feed_tasks)
    branch_partial = dot(gated, out_rel, 1, 0).astype(BF)
    (branch_partial,) = sync(feed_tasks, branch_partial)
    for task in feed_tasks:
        task.step()
    branch_sum = scatter_rows(branch_partial)
    (branch_sum,) = sync(feed_tasks, branch_sum)
    middle = inputs + branch_sum
    scaled_mid, inverse_mid = norm_parts(middle)
    second_own = spread((scaled_mid * feed_gain + feed_shift).astype(BF))
    second_own, upstream_parts = sync(feed_tasks, second_own, upstream_parts)
    second_parts = gather_start(second_own)
    for task in feed_tasks:
        task.step()
    upstream = gather_join(upstream_parts)
    hidden_grad = dot(upstream, down_rel, 1, 1)
    (second_parts,) = tie(second_parts)
    second_parts = gather_rest(second_parts)
    for task in feed_tasks:
        task.step()
    second_parts, hidden_grad = sync(feed_tasks, second_parts, hidden_grad)
    second = gather_join(second_parts)
    act_set, lin_set = pair_of_weights(act_task), pair_of_weights(lin_task)
    hidden, act_low, lin_low = [], [], []
    for j in (0, 1):
        active, linear = dot(second, act_set[j], 1, 0), dot(second, lin_set[j], 1, 0)
        upper = hidden_grad[:, j * h_set : (j + 1) * h_set]
        cdf = 0.5 * (1.0 + lax.erf(active * (2.0**-0.5)))
        gelu = active * cdf
        slope = cdf + active * jnp.exp(-0.5 * active * active) * (0.5 / jnp.pi) ** 0.5
        hidden.append((gelu * linear).astype(BF))
        act_low.append((upper * linear * slope).astype(BF))
        lin_low.append((upper * gelu).astype(BF))
    second_partial = (
        dot(act_low[0], act_set[0], 1, 1)
        + dot(act_low[1], act_set[1], 1, 1)
        + dot(lin_low[0], lin_set[0], 1, 1)
        + dot(lin_low[1], lin_set[1], 1, 1)
    ).astype(BF)
    second_partial, act_low, lin_low, hidden = tie(second_partial, act_low, lin_low, hidden)
    second_sum = scatter_rows(second_partial)
    act_grads = column_grads(second, act_low[0], act_low[1], (h_set,), False)
    lin_grads = column_grads(second, lin_low[0], lin_low[1], (h_set,), True)
    down_grads = row_grads(hidden[0], hidden[1], upstream, False)
    feed_grads = [act_grads, lin_grads]
    for task in feed_grads:
        task.step(2)
    down_grads.step()
    (second_sum,) = sync([*feed_grads, down_grads], second_sum)
    second_grad = unspread(second_sum)

    mid_term, grad_feed_gain, grad_feed_shift = norm_pull(
        scaled_mid, inverse_mid, feed_gain, second_grad
    )
    middle_grad = cotangent.astype(F32) + mid_term
    (branch_own,) = sync([*feed_grads, down_grads], middle_grad.astype(BF))
    branch_parts = gather_start(branch_own)
    for task in feed_grads:
        task.step()
    down_grads.step()
    (branch_parts,) = tie(branch_parts)
    branch_parts = gather_rest(branch_parts)
    down_partial = dot(jnp.concatenate(hidden, 1), down_rel, 1, 0).astype(BF)
    branch_parts, down_partial = sync([*feed_grads, down_grads], branch_parts, down_partial)
    branch = gather_join(branch_parts)
    for task in feed_grads:
        task.step()
    down_grads.step()

    gated_grad = dot(branch, out_rel, 1, 1)
    headed_low, shift_terms = [], []
    for j in (0, 1):
        upper = gated_grad[:, j * v_set : (j + 1) * v_set]
        shift_terms.append(upper * (gate_pre[j] * jax.nn.sigmoid(gate_pre[j])))
        headed_low.append((shift_terms[j] * gains[j]).astype(BF))
    headed_grad = heads_of(headed_low, VD)

    mixed_grads, terms = [], []
    for head in range(local_heads):
        _, query_factor, _, carry = tables[head]
        carried, later = None, [None] * spans
        for block in range(spans):
            at = head * spans + block
            upper = cut(headed_grad[head], block).astype(F32)
            normal = normal_all[at]
            mixed_grads.append(
                (
                    inv_all[at]
                    * (
                        upper
                        - jnp.mean(upper, -1, keepdims=True)
                        - normal * jnp.mean(upper * normal, -1, keepdims=True)
                    )
                ).astype(BF)
            )
        for block in reversed(range(spans)):
            later[block] = carried
            scaled_query = (cut(queries[head], block).astype(F32) * query_factor).astype(BF)
            term = dot(scaled_query, mixed_grads[head * spans + block], 0, 0)
            carried = term if carried is None else carried * carry + term
        terms.append((later, carried))
    leaving_low, gated_late, branch_late, gated_grad, shift_terms = tie(
        jnp.stack([term[1] for term in terms]).astype(BF), gated, branch, gated_grad, shift_terms
    )
    leaving_parts = state_start(leaving_low, -1)
    gate_low, group_sums = [], []
    for j in (0, 1):
        upper = gated_grad[:, j * v_set : (j + 1) * v_set]
        sigmoid = jax.nn.sigmoid(gate_pre[j])
        wide = headed[j].astype(F32)
        gate_low.append(
            (
                upper
                * (wide * gains[j] + biases[j])
                * (sigmoid * (1.0 + gate_pre[j] * (1.0 - sigmoid)))
            ).astype(BF)
        )
        group_sums.append((jnp.sum(shift_terms[j] * wide, 0), jnp.sum(shift_terms[j], 0)))
    out_grads = row_grads(gated_late[:, :v_set], gated_late[:, v_set:], branch_late, True)
    gate_grads = column_grads(normed, gate_low[0], gate_low[1], (v_set,), True)
    out_grads.step()
    gate_grads.step()
    middle_tasks = [*feed_grads, down_grads, out_grads, gate_grads]
    leaving_parts, gate_low = sync(middle_tasks, leaving_parts, gate_low)
    leaving = state_join(leaving_parts, decays**spans)
    for task in feed_grads:
        task.step()
    down_grads.step()

    query_grads, key_grads, value_grads = [], [], []
    for head in range(local_heads):
        inside, query_factor, key_factor, carry = tables[head]
        for block in range(spans):
            at = head * spans + block
            query, key, value = (cut(array[head], block) for array in (queries, keys, values))
            carried = leaving[head] * carry ** (spans - 1 - block)
            if terms[head][0][block] is not None:
                carried = carried + terms[head][0][block]
            carried_low = carried.astype(BF)
            score_grad = (dot(mixed_grads[at], value, 1, 1) * inside).astype(BF)
            query_grads.append(
                (
                    dot(score_grad, key, 1, 0)
                    + query_factor * dot(mixed_grads[at], state_all[at], 1, 1)
                ).astype(BF)
            )
            key_grads.append(
                (
                    dot(score_grad, query, 0, 0) + key_factor * dot(value, carried_low, 1, 1)
                ).astype(BF)
            )
            value_grads.append(
                (
                    dot(masked_all[at], mixed_grads[at], 0, 0)
                    + key_factor * dot(key, carried_low, 1, 0)
                ).astype(BF)
            )
    query_low, key_low, value_low = join(query_grads), join(key_grads), join(value_grads)
    query_key_low = [jnp.concatenate([query_low[j], key_low[j]], 1) for j in (0, 1)]
    normed_partial = (
        dot(value_low[0], value_set[0], 1, 1)
        + dot(value_low[1], value_set[1], 1, 1)
        + dot(query_key_low[0], query_key_set[0], 1, 1)
        + dot(query_key_low[1], query_key_set[1], 1, 1)
        + dot(gate_low[0], gate_set[0], 1, 1)
        + dot(gate_low[1], gate_set[1], 1, 1)
    ).astype(BF)
    normed_partial, value_low, query_key_low = sync(
        middle_tasks, normed_partial, value_low, query_key_low
    )
    normed_sum = scatter_rows(normed_partial)
    value_grads = column_grads(normed, value_low[0], value_low[1], (v_set,), False)
    query_key_grads = column_grads(
        normed, query_key_low[0], query_key_low[1], (q_set, q_set), True
    )
    last_grads = [value_grads, query_key_grads]
    for task in last_grads:
        task.step(2)
    out_grads.step()
    gate_grads.step()
    (normed_sum,) = sync([*last_grads, *middle_tasks], normed_sum)
    normed_grad = unspread(normed_sum)
    for task in last_grads:
        task.step()
    down_sum = scatter_rows(down_partial)
    for task in feed_grads:
        task.step()
    out_grads.step()
    gate_grads.step()
    down_grads.step()
    (down_sum,) = sync([*last_grads, *middle_tasks], down_sum)
    result = (middle + down_sum).astype(BF)
    for task in last_grads:
        task.step()
    for task in feed_grads:
        task.step()
    gate_grads.step()
    out_grads.step()
    down_grads.step()
    sync([*last_grads, *middle_tasks])
    for task in last_grads:
        task.step()
    for task in feed_grads:
        task.step()
    gate_grads.step()
    out_grads.step()
    sync([*last_grads, *middle_tasks])
    for task in last_grads:
        task.step()
    gate_grads.step()
    out_grads.step()
    sync([*last_grads, *middle_tasks])
    for task in last_grads:
        task.step()
    gate_grads.step()
    (grad_act,), (grad_lin,), (grad_down,) = (task.finish() for task in [*feed_grads, down_grads])
    (grad_out,), (grad_gate,) = out_grads.finish(), gate_grads.finish()
    sync(last_grads)
    (grad_value,), (grad_query, grad_key) = (task.finish() for task in last_grads)
    in_term, grad_mixer_gain, grad_mixer_shift = norm_pull(
        scaled_in, inverse_in, mixer_gain, normed_grad
    )
    grad_tokens = (middle_grad + in_term).astype(BF)

    def placed(parts):
        out = jnp.zeros(group_gain.shape, F32)
        for j in (0, 1):
            out = lax.dynamic_update_slice_in_dim(
                out, parts[j], (2 * place + (core ^ j)) * v_set, 0
            )
        return out

    def total(parts):
        sizes = [part.shape[0] for part in parts]
        packed = sum_everywhere(jnp.concatenate(parts).reshape(-1, 128)).reshape(-1)
        outs, start = [], 0
        for size in sizes:
            outs.append(packed[start : start + size])
            start += size
        return outs

    grad_group_gain, grad_group_shift, grad_feed_gain, grad_feed_shift = total(
        [
            placed([sums[0] for sums in group_sums]),
            placed([sums[1] for sums in group_sums]),
            grad_feed_gain,
            grad_feed_shift,
        ]
    )
    grad_mixer_gain, grad_mixer_shift = total([grad_mixer_gain, grad_mixer_shift])
    return (
        result,
        grad_tokens,
        grad_query,
        grad_key,
        grad_value,
        grad_gate,
        grad_out,
        grad_act,
        grad_lin,
        grad_down,
        grad_mixer_gain,
        grad_mixer_shift,
        grad_group_gain,
        grad_group_shift,
        grad_feed_gain,
        grad_feed_shift,
    )


def solution(mesh):
    rows = P(("dp", "seq", "fsdp"), None)
    shard = P("fsdp", None)
    return jax.shard_map(
        on_device,
        mesh=mesh,
        in_specs=(rows, P(), P())
        + (shard,) * 4
        + (P(), P(), P(), shard, P(), P())
        + (shard,) * 3
        + (rows,),
        out_specs=(rows, rows) + (shard,) * 8 + (P(),) * 6,
        check_vma=False,
    )
```

```python
import jax
import jax.numpy as jnp
from jax import lax
from jax.experimental import pallas as pl
from jax.experimental.pallas import tpu as pltpu
from jax.sharding import PartitionSpec as P

H = 8
KD = 256
VD = 512
SPAN = 512
EPSILON = 1e-05
BF = jnp.bfloat16
F32 = jnp.float32


def norm_parts(values):
    center = values - jnp.mean(values, -1, keepdims=True)
    inverse = lax.rsqrt(jnp.mean(center * center, -1, keepdims=True) + EPSILON)
    return center * inverse, inverse


def norm_pull(scaled, inverse, gain, grad):
    lifted = grad * gain
    term = inverse * (
        lifted
        - jnp.mean(lifted, -1, keepdims=True)
        - scaled * jnp.mean(lifted * scaled, -1, keepdims=True)
    )
    return term, jnp.sum(grad * scaled, 0), jnp.sum(grad, 0)


def dot(left, right, left_axis, right_axis):
    return lax.dot_general(
        left, right, (((left_axis,), (right_axis,)), ((), ())), preferred_element_type=F32
    )


def after(values, *others):
    return lax.optimization_barrier((values, *others))[0]


def shift(values, axis, step):
    count = lax.axis_size(axis)
    return lax.ppermute(values, axis, [(i, (i + step) % count) for i in range(count)])


def pass_on(values, axis, step):
    count = lax.axis_size(axis)
    pairs = [(i, i + step) for i in range(count) if 0 <= i + step < count]
    return lax.ppermute(values, axis, pairs)


def swap(values, axis, mask):
    return lax.ppermute(values, axis, [(i, i ^ mask) for i in range(lax.axis_size(axis))])


def tie(*trees):
    return lax.optimization_barrier(trees)


def slot_offsets():
    count = lax.axis_size("fsdp")
    return [0, -1, 1, 2] if count == 4 else [0] + [-k for k in range(1, count)]


def gather_start(values):
    count = lax.axis_size("fsdp")
    if count == 4:
        return [values, pass_on(values, "fsdp", 1), pass_on(values, "fsdp", -1)]
    return [values] + [shift(values, "fsdp", k) for k in range(1, count)]


def gather_rest(parts):
    if lax.axis_size("fsdp") != 4:
        return parts
    place = lax.axis_index("fsdp")
    own, below, above = parts
    far_down = lax.ppermute(above, "fsdp", [(1, 0), (2, 1)])
    far_up = lax.ppermute(below, "fsdp", [(1, 2), (2, 3)])
    ends = lax.ppermute(jnp.where(place == 2, above, below), "fsdp", [(2, 0), (1, 3)])
    return [own, below, above, far_down, far_up, ends]


def gather_join(parts):
    if lax.axis_size("fsdp") != 4:
        return jnp.concatenate(parts, 0)
    place = lax.axis_index("fsdp")
    own, below, above, far_down, far_up, ends = parts
    return jnp.concatenate(
        [
            own,
            jnp.where(place == 0, ends, below),
            jnp.where(place == 3, ends, above),
            jnp.where(place < 2, far_down, far_up),
        ],
        0,
    )


def gather_rows(values):
    return gather_join(gather_rest(gather_start(values)))


def scatter_start(low):
    count = lax.axis_size("fsdp")
    rows = low.shape[0] // count
    parts = [low[k * rows : (k + 1) * rows] for k in range(count)]
    if count != 4:
        return parts[:1] + [shift(parts[k], "fsdp", -k) for k in range(1, count)]
    place = lax.axis_index("fsdp")
    own, below, above, far = parts
    from_below = lax.ppermute(far, "fsdp", [(0, 1), (1, 2)])
    from_above = lax.ppermute(far, "fsdp", [(2, 1), (3, 2)])
    ends = lax.ppermute(jnp.where(place == 0, below, above), "fsdp", [(0, 2), (3, 1)])
    return [own, below, above, from_below, from_above, ends]


def scatter_rest(parts):
    if lax.axis_size("fsdp") != 4:
        return parts
    place = lax.axis_index("fsdp")
    own, below, above, from_below, from_above, ends = parts
    ends = ends.astype(F32)
    up = above.astype(F32) + from_below.astype(F32) + jnp.where(place == 2, ends, 0.0)
    down = below.astype(F32) + from_above.astype(F32) + jnp.where(place == 1, ends, 0.0)
    return [own, pass_on(up.astype(BF), "fsdp", 1), pass_on(down.astype(BF), "fsdp", -1)]


def scatter_join(parts):
    total = parts[0].astype(F32)
    for part in parts[1:]:
        total = total + part.astype(F32)
    return total


def exchange(piece):
    count = lax.axis_size("fsdp")
    place = lax.axis_index("fsdp")
    return [piece(place)] + [shift(piece((place - k) % count), "fsdp", -k) for k in range(1, count)]


def in_order(pieces):
    count = len(pieces)
    stacked = jnp.stack(pieces + pieces[:-1])
    place = lax.axis_index("fsdp")
    return lax.dynamic_slice_in_dim(stacked, (count - place) % count, count, 0)


def stages():
    masks = []
    for axis, first in (("seq", 2), ("dp", 1)):
        mask = first
        while mask < lax.axis_size(axis):
            masks.append((axis, mask))
            mask *= 2
    return masks


def stage_bits():
    return [(lax.axis_index(axis) // mask) % 2 for axis, mask in stages()]


def quarter_count():
    return 2 ** len(stages())


def quarter_place():
    place = jnp.int32(0)
    for bit in stage_bits():
        place = place * 2 + bit
    return place


def core_place():
    return lax.axis_index("seq") % 2


class Task:
    def __init__(self, values, steps):
        self.values, self.steps = values, list(steps)

    def step(self, times=1):
        for _ in range(times):
            self.values = self.steps.pop(0)(self.values)

    def finish(self):
        self.step(len(self.steps))
        return self.values


def hold(tasks, *trees):
    firsts, trees = lax.optimization_barrier(([task.values[0] for task in tasks], trees))
    for task, held in zip(tasks, firsts):
        task.values = [held, *task.values[1:]]
    return trees


def sync(tasks, *trees):
    values, trees = lax.optimization_barrier(([task.values for task in tasks], trees))
    for task, held in zip(tasks, values):
        task.values = held
    return trees


def gather_steps(flipped, ready):
    chain = stages()
    order = list(range(len(chain)))
    order = order if flipped else order[::-1]
    held = []

    def send(at):
        def run(values):
            axis, mask = chain[at]
            return [values, swap(values, axis, mask), at]

        return run

    def join(values):
        mine, arrived, at = values
        spot = sum(other < at for other in held)
        held.append(at)
        return jnp.stack([mine, arrived], spot)

    def first(values):
        return send(order[0])(ready(values))[:2]

    def second(values):
        now = join([*values, order[0]])
        for at in order[1:-1]:
            now = join(send(at)(now))
        return send(order[-1])(now)[:2]

    def third(values):
        now = join([*values, order[-1]])
        now = now.reshape(quarter_count(), *now.shape[len(held) :])
        return [now, swap(now, "seq", 1)]

    return [first, second, third]


def reduce_steps(own_part, flipped, absolute):
    chain = stages()
    order = list(range(len(chain)))
    order = order[::-1] if flipped else order
    left = list(range(len(chain)))

    def split(values, at):
        axis, mask = chain[at]
        spot = left.index(at)
        left.remove(at)
        if absolute:
            bit = (lax.axis_index(axis) // mask) % 2
            keep = lax.dynamic_index_in_dim(values, bit, spot, False)
            send = lax.dynamic_index_in_dim(values, 1 - bit, spot, False)
        else:
            keep = lax.index_in_dim(values, 0, spot, False)
            send = lax.index_in_dim(values, 1, spot, False)
        return [keep, swap(send, axis, mask)]

    def add(values):
        return (values[0].astype(F32) + values[1].astype(F32)).astype(BF)

    def core(values):
        return [swap(values[0], "seq", 1)]

    def first(values):
        both = (own_part() + values[0].astype(F32)).astype(BF)
        count = lax.axis_size("fsdp")
        if absolute:
            tail = (both.shape[0] // quarter_count(), both.shape[1])
        else:
            tail = (count, both.shape[0] // (quarter_count() * count), both.shape[1])
        return split(both.reshape(*([2] * len(chain)), *tail), order[0])

    def second(values):
        now = add(values)
        for at in order[1:-1]:
            now = add(split(now, at))
        return split(now, order[-1])

    return [core, first, second], add


def weight_task(weights, flipped):
    count = lax.axis_size("fsdp")
    rows = weights[0].shape[0] // quarter_count()
    core = core_place()
    own = [lax.dynamic_slice_in_dim(w, quarter_place() * rows, rows, 0) for w in weights]

    def piece(target):
        parts = []
        for w in own:
            width = w.shape[1] // (2 * count)
            parts.append(lax.dynamic_slice_in_dim(w, (2 * target + core) * width, width, 1))
        return jnp.concatenate(parts, 1)

    return Task(exchange(piece), gather_steps(flipped, in_order))


def pair_of_weights(task):
    return [part.reshape(-1, part.shape[-1]) for part in task.values]


def column_grads(left, own, other, widths, flipped):
    steps, add = reduce_steps(lambda: dot(left, own, 0, 0), flipped, False)

    def across(values):
        summed = add(values)
        return exchange(lambda target: lax.dynamic_index_in_dim(summed, target, 0, False))

    def out(values):
        return place_columns(values[0], values[1], widths)

    return Task(
        [dot(left, other, 0, 0).astype(BF)],
        [*steps, across, *gather_steps(flipped, jnp.stack), out],
    )


def place_columns(own, other, widths):
    quarters, count, rows, _ = own.shape
    places = jnp.stack([quarter_place(), core_place(), lax.axis_index("fsdp")])

    def body(place_ref, own_ref, other_ref, *out_refs):
        first = place_ref[1] == 0
        start = 0
        for out_ref, width in zip(out_refs, widths):
            spot = slice(start, start + width)

            @pl.when(first)
            def _():
                out_ref[0, :, :width] = own_ref[0, 0, :, spot].astype(F32)
                out_ref[0, :, width:] = other_ref[0, 0, :, spot].astype(F32)

            @pl.when(jnp.logical_not(first))
            def _():
                out_ref[0, :, :width] = other_ref[0, 0, :, spot].astype(F32)
                out_ref[0, :, width:] = own_ref[0, 0, :, spot].astype(F32)

            start += width

    block = pl.BlockSpec((1, 1, rows, own.shape[3]), lambda q, z, place: (q, z, 0, 0))
    outs = pl.pallas_call(
        body,
        grid_spec=pltpu.PrefetchScalarGridSpec(
            num_scalar_prefetch=1,
            grid=(quarters, count),
            in_specs=[block, block],
            out_specs=[
                pl.BlockSpec(
                    (1, rows, 2 * width),
                    lambda q, z, place: (q ^ place[0], 0, lax.rem(z + place[2], count)),
                )
                for width in widths
            ],
        ),
        out_shape=[
            jax.ShapeDtypeStruct((quarters, rows, 2 * width * count), F32) for width in widths
        ],
        cost_estimate=pl.CostEstimate(flops=0, bytes_accessed=own.size * 12, transcendentals=0),
    )(places, own, other)
    return [out.reshape(quarters * rows, out.shape[2]) for out in outs]


def row_grads(own, other, right):
    first = core_place() == 0
    left = jnp.concatenate([jnp.where(first, own, other), jnp.where(first, other, own)], 1)
    return lax.psum(dot(left, right, 0, 0).astype(BF), ("dp", "seq"))


def swap_quarters(pieces):
    bits = stage_bits()
    for at, bit in enumerate(bits):
        mask = 1 << (len(bits) - 1 - at)
        pieces = [jnp.where(bit == 1, pieces[c ^ mask], pieces[c]) for c in range(len(pieces))]
    return pieces


def spread(values):
    count, quarters = lax.axis_size("fsdp"), quarter_count()
    chunk = values.shape[1] // (count * quarters)
    groups = []
    for z in range(count):
        starts = [(z * quarters + q) * chunk for q in range(quarters)]
        groups.append(swap_quarters([values[:, s : s + chunk] for s in starts]))
    return jnp.concatenate([groups[z][q] for q in range(quarters) for z in range(count)], 1)


def unspread(values):
    count, quarters = lax.axis_size("fsdp"), quarter_count()
    chunk = values.shape[1] // (count * quarters)
    outs = []
    for z in range(count):
        starts = [(q * count + z) * chunk for q in range(quarters)]
        outs += swap_quarters([values[:, s : s + chunk] for s in starts])
    return jnp.concatenate(outs, 1)


def flip_state(states):
    if states.shape[0] % 2 == 0:
        half = states.shape[0] // 2
        return jnp.concatenate([states[half:], states[:half]], 0)
    half_k, half_v = states.shape[1] // 2, states.shape[2] // 2
    turned = jnp.concatenate([states[:, half_k:], states[:, :half_k]], 1)
    return jnp.concatenate([turned[:, :, half_v:], turned[:, :, :half_v]], 2)


def state_start(own, sign):
    count = lax.axis_size("seq")
    low = own.astype(BF)
    flipped = flip_state(low)
    return [pass_on(flipped if k % 2 else low, "seq", sign * k) for k in range(1, count)]


def state_join(parts, decay):
    total = parts[0].astype(F32)
    for k, part in enumerate(parts[1:], 1):
        total = total + part.astype(F32) * decay**k
    return total


def on_device(
    tokens,
    mixer_gain,
    mixer_shift,
    w_query,
    w_key,
    w_value,
    w_gate,
    decay_exponent,
    group_gain,
    group_shift,
    w_out,
    feed_gain,
    feed_shift,
    w_act,
    w_lin,
    w_down,
    cotangent,
):
    count = lax.axis_size("fsdp")
    place = lax.axis_index("fsdp")
    core = core_place()
    rows = tokens.shape[0]
    group = rows * count
    spans = group // SPAN
    local_heads = H // count
    q_set, v_set = local_heads * KD // 2, local_heads * VD // 2
    h_set = w_act.shape[1] // (2 * count)
    key_scale = KD ** (-0.5)

    def natural(values):
        if spans == 1:
            return values
        blocks = values.reshape(count, rows, values.shape[1])
        pieces = [blocks[0]] + [blocks[count - k] for k in range(1, count)]
        return in_order(pieces).reshape(values.shape)

    def relative(values):
        if spans == 1:
            return values
        blocks = values.reshape(count, rows, values.shape[1])
        doubled = jnp.concatenate([blocks, blocks[:-1]])
        turned = lax.dynamic_slice_in_dim(doubled, place, count, 0)
        return jnp.stack([turned[0]] + [turned[count - k] for k in range(1, count)]).reshape(
            values.shape
        )

    def own_rows(weight):
        half = weight.shape[0] // 2
        return jnp.concatenate(
            [lax.dynamic_slice_in_dim(weight, (core ^ j) * half, half, 0) for j in (0, 1)], 0
        )

    def heads_of(pair, width):
        if local_heads % 2:
            return [natural(jnp.concatenate(pair, 1))]
        return [
            natural(part)[:, i * width : (i + 1) * width]
            for part in pair
            for i in range(local_heads // 2)
        ]

    def pair_of(heads):
        if local_heads % 2:
            half = heads[0].shape[1] // 2
            return relative(heads[0][:, :half]), relative(heads[0][:, half:])
        half = len(heads) // 2
        return tuple(
            relative(jnp.concatenate(heads[j * half : (j + 1) * half], 1)) for j in (0, 1)
        )

    if local_heads % 2:
        head_places = [place]
    else:
        half_heads = local_heads // 2
        head_places = [
            place * local_heads + (core ^ j) * half_heads + i
            for j in (0, 1)
            for i in range(half_heads)
        ]

    inputs = tokens.astype(F32)
    value_task = weight_task((w_value,), False)
    query_key_task = weight_task((w_query, w_key), True)
    scaled_in, inverse_in = norm_parts(inputs)
    normed_own = spread((scaled_in * mixer_gain + mixer_shift).astype(BF))
    first_tasks = [value_task, query_key_task]
    normed_own, free_gate = sync(first_tasks, normed_own, w_gate)
    gate_task = weight_task((free_gate,), True)
    for task in first_tasks:
        task.step()
    (normed_own,) = sync([*first_tasks, gate_task], normed_own)
    for task in first_tasks:
        task.step()
    normed_parts = gather_start(normed_own)
    (normed_parts,) = tie(normed_parts)
    normed_parts = gather_rest(normed_parts)
    sync(first_tasks)
    (gate_values,) = tie(gate_task.values)
    for task in first_tasks:
        task.step()
    gate_task.step()
    normed_parts, late = sync([gate_task], normed_parts, (w_act, w_lin))
    normed = gather_join(normed_parts)
    value_set, query_key_set = pair_of_weights(value_task), pair_of_weights(query_key_task)
    gate_task.step()
    act_task, lin_task = weight_task((late[0],), False), weight_task((late[1],), True)
    feed_tasks = [act_task, lin_task]
    out_rel, down_rel = own_rows(w_out), own_rows(w_down)

    log_rates = jnp.log1p(-jnp.exp2(-decay_exponent.astype(F32)))
    if spans == 1:
        index = jnp.arange(SPAN)
        steps = jnp.zeros(SPAN, jnp.int32)
        for slot, offset in enumerate(slot_offsets()):
            steps = jnp.where(index // rows == slot, offset, steps)
        positions = ((place + steps + count) % count * rows + index % rows).astype(F32)
    else:
        positions = jnp.arange(SPAN).astype(F32)
    offsets = positions[:, None] - positions[None, :]
    tables = []
    for at in head_places:
        log_rate = lax.dynamic_index_in_dim(log_rates, at, 0, False)
        inside = (
            jnp.where(offsets >= 0, jnp.exp(jnp.maximum(offsets, 0.0) * log_rate), 0.0) * key_scale
        )
        tables.append(
            (
                inside,
                key_scale * jnp.exp((positions + 1.0) * log_rate)[:, None],
                jnp.exp((SPAN - 1.0 - positions) * log_rate)[:, None],
                jnp.exp(SPAN * log_rate),
            )
        )
    decays = jnp.stack([table[3] for table in tables])[:, None, None]

    value_pair = [dot(normed, part, 1, 0).astype(BF) for part in value_set]
    query_key_pair = [dot(normed, part, 1, 0).astype(BF) for part in query_key_set]
    keys = heads_of([part[:, q_set:] for part in query_key_pair], KD)
    values = heads_of(value_pair, VD)
    queries = heads_of([part[:, :q_set] for part in query_key_pair], KD)

    def cut(array, block):
        return array[block * SPAN : (block + 1) * SPAN]

    local_states, finals = [], []
    for head in range(local_heads):
        _, _, key_factor, carry = tables[head]
        state, states = None, []
        for block in range(spans):
            scaled_keys = (cut(keys[head], block).astype(F32) * key_factor).astype(BF)
            update = dot(scaled_keys, cut(values[head], block), 0, 0)
            states.append(state)
            state = update if state is None else state * carry + update
        local_states.append(states)
        finals.append(state)
    entering_parts = state_start(jnp.stack(finals), 1)
    (upstream_own,) = sync(feed_tasks, cotangent)
    upstream_parts = gather_start(upstream_own)
    entering_parts, upstream_parts = sync([gate_task], entering_parts, upstream_parts)
    upstream_parts = gather_rest(upstream_parts)
    entering = state_join(entering_parts, decays**spans)
    gate_task.step()
    for task in feed_tasks:
        task.step()
    gate_set = pair_of_weights(gate_task)
    gate_pre = [dot(normed, part, 1, 0) for part in gate_set]

    masked_all, state_all, normal_all, inv_all = [], [], [], []
    for head in range(local_heads):
        inside, query_factor, _, carry = tables[head]
        for block in range(spans):
            query = cut(queries[head], block)
            masked = (dot(query, cut(keys[head], block), 1, 1) * inside).astype(BF)
            state = entering[head] * carry**block
            if local_states[head][block] is not None:
                state = state + local_states[head][block]
            state_low = state.astype(BF)
            mixed = dot(masked, cut(values[head], block), 1, 0) + query_factor * dot(
                query, state_low, 1, 0
            )
            mean = jnp.mean(mixed, -1, keepdims=True)
            inv_std = lax.rsqrt(jnp.mean(mixed * mixed, -1, keepdims=True) - mean * mean + EPSILON)
            masked_all.append(masked)
            state_all.append(state_low)
            normal_all.append((mixed - mean) * inv_std)
            inv_all.append(inv_std)

    def join(parts):
        return pair_of(
            [
                jnp.concatenate(parts[head * spans : (head + 1) * spans], 0)
                for head in range(local_heads)
            ]
        )

    headed = join([normal.astype(BF) for normal in normal_all])
    gains, biases = [], []
    for j in (0, 1):
        start = (2 * place + (core ^ j)) * v_set
        gains.append(lax.dynamic_slice_in_dim(group_gain, start, v_set, 0))
        biases.append(lax.dynamic_slice_in_dim(group_shift, start, v_set, 0))
    silus = [gate * jax.nn.sigmoid(gate) for gate in gate_pre]
    gated = jnp.concatenate(
        [
            (silus[j] * (headed[j].astype(F32) * gains[j] + biases[j])).astype(BF)
            for j in (0, 1)
        ],
        1,
    )

    branch_parts = scatter_start(dot(gated, out_rel, 1, 0).astype(BF))
    (branch_parts,) = sync(feed_tasks, branch_parts)
    branch_parts = scatter_rest(branch_parts)
    for task in feed_tasks:
        task.step()
    middle = inputs + scatter_join(branch_parts)
    scaled_mid, inverse_mid = norm_parts(middle)
    second_own = spread((scaled_mid * feed_gain + feed_shift).astype(BF))
    second_own, upstream_parts = tie(second_own, upstream_parts)
    second_parts = gather_start(second_own)
    upstream = gather_join(upstream_parts)
    hidden_grad = dot(upstream, down_rel, 1, 1)
    (second_parts,) = sync(feed_tasks, second_parts)
    second_parts = gather_rest(second_parts)
    for task in feed_tasks:
        task.step()
    second_parts, hidden_grad = sync(feed_tasks, second_parts, hidden_grad)
    second = gather_join(second_parts)
    act_set, lin_set = pair_of_weights(act_task), pair_of_weights(lin_task)
    hidden, act_low, lin_low = [], [], []
    for j in (0, 1):
        active, linear = dot(second, act_set[j], 1, 0), dot(second, lin_set[j], 1, 0)
        upper = hidden_grad[:, j * h_set : (j + 1) * h_set]
        cdf = 0.5 * (1.0 + lax.erf(active * (2.0**-0.5)))
        gelu = active * cdf
        slope = cdf + active * jnp.exp(-0.5 * active * active) * (0.5 / jnp.pi) ** 0.5
        hidden.append((gelu * linear).astype(BF))
        act_low.append((upper * linear * slope).astype(BF))
        lin_low.append((upper * gelu).astype(BF))
    second_partial = (
        dot(act_low[0], act_set[0], 1, 1)
        + dot(act_low[1], act_set[1], 1, 1)
        + dot(lin_low[0], lin_set[0], 1, 1)
        + dot(lin_low[1], lin_set[1], 1, 1)
    ).astype(BF)
    second_partial, act_low, lin_low, hidden = tie(second_partial, act_low, lin_low, hidden)
    second_parts = scatter_start(second_partial)
    act_grads = column_grads(second, act_low[0], act_low[1], (h_set,), False)
    lin_grads = column_grads(second, lin_low[0], lin_low[1], (h_set,), True)
    feed_grads = [act_grads, lin_grads]
    for task in feed_grads:
        task.step(2)
    down_summed = row_grads(hidden[0], hidden[1], upstream)
    (second_parts,) = hold(feed_grads, second_parts)
    second_grad = unspread(scatter_join(scatter_rest(second_parts)))

    mid_term, grad_feed_gain, grad_feed_shift = norm_pull(
        scaled_mid, inverse_mid, feed_gain, second_grad
    )
    middle_grad = cotangent.astype(F32) + mid_term
    (branch_own,) = sync(feed_grads, middle_grad.astype(BF))
    branch_parts = gather_start(branch_own)
    for task in feed_grads:
        task.step()
    (branch_parts,) = sync(feed_grads, branch_parts)
    branch_parts = gather_rest(branch_parts)
    down_partial = dot(jnp.concatenate(hidden, 1), down_rel, 1, 0).astype(BF)
    (branch_parts,) = tie(branch_parts)
    branch = gather_join(branch_parts)
    hold(feed_grads, branch)
    for task in feed_grads:
        task.step()

    gated_grad = dot(branch, out_rel, 1, 1)
    headed_low, shift_terms = [], []
    for j in (0, 1):
        upper = gated_grad[:, j * v_set : (j + 1) * v_set]
        shift_terms.append(upper * (gate_pre[j] * jax.nn.sigmoid(gate_pre[j])))
        headed_low.append((shift_terms[j] * gains[j]).astype(BF))
    headed_grad = heads_of(headed_low, VD)

    mixed_grads, terms = [], []
    for head in range(local_heads):
        _, query_factor, _, carry = tables[head]
        carried, later = None, [None] * spans
        for block in range(spans):
            at = head * spans + block
            upper = cut(headed_grad[head], block).astype(F32)
            normal = normal_all[at]
            mixed_grads.append(
                (
                    inv_all[at]
                    * (
                        upper
                        - jnp.mean(upper, -1, keepdims=True)
                        - normal * jnp.mean(upper * normal, -1, keepdims=True)
                    )
                ).astype(BF)
            )
        for block in reversed(range(spans)):
            later[block] = carried
            scaled_query = (cut(queries[head], block).astype(F32) * query_factor).astype(BF)
            term = dot(scaled_query, mixed_grads[head * spans + block], 0, 0)
            carried = term if carried is None else carried * carry + term
        terms.append((later, carried))
    leaving_low, gated_late, branch_late, gated_grad, shift_terms = tie(
        jnp.stack([term[1] for term in terms]).astype(BF), gated, branch, gated_grad, shift_terms
    )
    leaving_parts = state_start(leaving_low, -1)
    gate_low, group_sums = [], []
    for j in (0, 1):
        upper = gated_grad[:, j * v_set : (j + 1) * v_set]
        sigmoid = jax.nn.sigmoid(gate_pre[j])
        wide = headed[j].astype(F32)
        gate_low.append(
            (
                upper
                * (wide * gains[j] + biases[j])
                * (sigmoid * (1.0 + gate_pre[j] * (1.0 - sigmoid)))
            ).astype(BF)
        )
        group_sums.append((jnp.sum(shift_terms[j] * wide, 0), jnp.sum(shift_terms[j], 0)))
    gate_grads = column_grads(normed, gate_low[0], gate_low[1], (v_set,), True)
    gate_grads.step(2)
    (leaving_parts,) = sync(feed_grads, leaving_parts)
    leaving = state_join(leaving_parts, decays**spans)
    for task in feed_grads:
        task.step()
    (down_partial,) = tie(down_partial, leaving)[:1]
    down_parts = scatter_start(down_partial)
    gated_late, branch_late, _ = tie(gated_late, branch_late, down_summed)
    out_summed = row_grads(gated_late[:, :v_set], gated_late[:, v_set:], branch_late)

    query_grads, key_grads, value_grads = [], [], []
    for head in range(local_heads):
        inside, query_factor, key_factor, carry = tables[head]
        for block in range(spans):
            at = head * spans + block
            query, key, value = (cut(array[head], block) for array in (queries, keys, values))
            carried = leaving[head] * carry ** (spans - 1 - block)
            if terms[head][0][block] is not None:
                carried = carried + terms[head][0][block]
            carried_low = carried.astype(BF)
            score_grad = (dot(mixed_grads[at], value, 1, 1) * inside).astype(BF)
            query_grads.append(
                (
                    dot(score_grad, key, 1, 0)
                    + query_factor * dot(mixed_grads[at], state_all[at], 1, 1)
                ).astype(BF)
            )
            key_grads.append(
                (
                    dot(score_grad, query, 0, 0) + key_factor * dot(value, carried_low, 1, 1)
                ).astype(BF)
            )
            value_grads.append(
                (
                    dot(masked_all[at], mixed_grads[at], 0, 0)
                    + key_factor * dot(key, carried_low, 1, 0)
                ).astype(BF)
            )
    query_low, key_low, value_low = join(query_grads), join(key_grads), join(value_grads)
    query_key_low = [jnp.concatenate([query_low[j], key_low[j]], 1) for j in (0, 1)]
    normed_partial = (
        dot(value_low[0], value_set[0], 1, 1)
        + dot(value_low[1], value_set[1], 1, 1)
        + dot(query_key_low[0], query_key_set[0], 1, 1)
        + dot(query_key_low[1], query_key_set[1], 1, 1)
        + dot(gate_low[0], gate_set[0], 1, 1)
        + dot(gate_low[1], gate_set[1], 1, 1)
    ).astype(BF)
    normed_partial, value_low, query_key_low = sync(
        [*feed_grads, gate_grads], normed_partial, value_low, query_key_low
    )
    normed_parts = scatter_start(normed_partial)
    value_grads = column_grads(normed, value_low[0], value_low[1], (v_set,), False)
    query_key_grads = column_grads(
        normed, query_key_low[0], query_key_low[1], (q_set, q_set), True
    )
    last_grads = [value_grads, query_key_grads]
    for task in [*feed_grads, gate_grads]:
        task.step()
    for task in last_grads:
        task.step(2)
    normed_parts, down_parts = hold(last_grads, normed_parts, down_parts)
    normed_parts = scatter_rest(normed_parts)
    (normed_parts,) = sync([*feed_grads, gate_grads], normed_parts)
    normed_grad = unspread(scatter_join(normed_parts))
    for task in [*feed_grads, gate_grads]:
        task.step()
    down_parts = scatter_rest(down_parts)
    sync(last_grads)
    for task in last_grads:
        task.step()
    sync([*last_grads, *feed_grads, gate_grads])
    for task in last_grads:
        task.step()
    gate_grads.step()
    (grad_act,), (grad_lin,) = (task.finish() for task in feed_grads)
    result = (middle + scatter_join(down_parts)).astype(BF)
    sync([*last_grads, gate_grads])
    for task in [*last_grads, gate_grads]:
        task.step()
    sync([*last_grads, gate_grads])
    for task in [*last_grads, gate_grads]:
        task.step()
    sync([*last_grads, gate_grads])
    (grad_gate,) = gate_grads.finish()
    (grad_value,), (grad_query, grad_key) = (task.finish() for task in last_grads)
    grad_down, grad_out = down_summed.astype(F32), out_summed.astype(F32)
    in_term, grad_mixer_gain, grad_mixer_shift = norm_pull(
        scaled_in, inverse_in, mixer_gain, normed_grad
    )
    grad_tokens = (middle_grad + in_term).astype(BF)

    def placed(parts):
        out = jnp.zeros(group_gain.shape, F32)
        for j in (0, 1):
            out = lax.dynamic_update_slice_in_dim(
                out, parts[j], (2 * place + (core ^ j)) * v_set, 0
            )
        return out

    vectors = lax.psum(
        jnp.concatenate(
            [
                grad_mixer_gain,
                grad_mixer_shift,
                placed([sums[0] for sums in group_sums]),
                placed([sums[1] for sums in group_sums]),
                grad_feed_gain,
                grad_feed_shift,
            ]
        ).reshape(-1, 128),
        ("dp", "seq", "fsdp"),
    ).reshape(-1)
    width, wide = mixer_gain.shape[0], group_gain.shape[0]
    marks = [width, 2 * width, 2 * width + wide, 2 * width + 2 * wide, 3 * width + 2 * wide]
    small = jnp.split(vectors, marks)
    return (
        result,
        grad_tokens,
        grad_query,
        grad_key,
        grad_value,
        grad_gate,
        grad_out,
        grad_act,
        grad_lin,
        grad_down,
        *small,
    )


def solution(mesh):
    rows = P(("dp", "seq", "fsdp"), None)
    shard = P("fsdp", None)
    return jax.shard_map(
        on_device,
        mesh=mesh,
        in_specs=(rows, P(), P())
        + (shard,) * 4
        + (P(), P(), P(), shard, P(), P())
        + (shard,) * 3
        + (rows,),
        out_specs=(rows, rows) + (shard,) * 8 + (P(),) * 6,
        check_vma=False,
    )
```
